32 devices in a mesh: req: 4 (over z), seq: 8 (over y, x, core).
Axes of the slice: x: 2, y: 2, z: 4, core: 2. Of those that a mesh axis runs over, the one named last changes fastest.
Arguments:
- q_nope: bfloat16 [2, 8, 128, 128], P(None, None, 'req'), may hold values from -16 to 16
- q_rope: bfloat16 [2, 8, 128, 64], P(None, None, 'req'), may hold values from -16 to 16
- w_uk: bfloat16 [128, 128, 512], P('req'), may hold values from -0.5 to 0.5
- w_uv: bfloat16 [128, 512, 128], P('req'), may hold values from -0.25 to 0.25
- latent_cache: bfloat16 [8, 49152, 512], P('req', 'seq'), may hold values from -120 to 120, as said below
- rope_cache: bfloat16 [8, 49152, 64], P('req', 'seq'), may hold values from -6 to 6
- positions: int32 [8, 49152], P('req', 'seq'), may hold values from 0 to 98303, as said below
- new_latent: bfloat16 [2, 8, 512], replicated, may hold values from -12 to 12
- new_rope: bfloat16 [2, 8, 64], replicated, may hold values from -6 to 6
- new_pos: int32 [8], replicated, may hold values from 98304 to 102399
- lengths: int32 [8], replicated, may hold values from 8192 to 49152, as said below
- assignment: int32 [8], replicated, may hold values from 0 to 7, each once
Outputs:
- attn_out: bfloat16 [2, 8, 128, 128], P(None, None, 'req')
The draws below stay inside these ranges and needn't reach their ends.
Inputs may be any that keep to these rules, and one draw needn't show every extreme that they name: lengths are given by request; the longest request uses all 49152 rows. Within each slot the positions rise strictly along the rows, by 1 or 2 a row, starting at 0 or 1; some slot rises by 2 on every row and ends at the largest value, some slot starts at 0. `new_pos`: each request's new positions exceed every cached position. `assignment`: a permutation; slots g * 2 to (g + 1) * 2 - 1 form request group g. `latent_cache`: entries lie within the given bounds.
All inputs are finite; a program needn't handle non-finite values.
Results may differ from the reference program's by a relative error of at most 0.0085.
The reference program's roundings to bfloat16 on the way count: a program that leaves them out, or rounds other values in their place, can miss the bound.
Values may be sent and summed in bfloat16 or wider, within the bound.
No kernel may reach another device: no remote copies, remote signals or barrier semaphores. Data moves between devices by JAX's collectives and lax.ppermute only.
A program may use at most 192 MiB of HBM per device.

```python
import math
import jax
import jax.numpy as jnp
from jax import lax

H = 128
DL = 512
DR = 64
DN = 128
DV = 128
STEPS = 2
REQS = 8
LMAX = 49152


def draw_lengths(key, part):
    first_key, second_key = jax.random.split(key)
    drawn = jax.random.randint(first_key, (REQS,), LMAX // 6, LMAX + 1)
    chosen = jax.random.randint(second_key, (), 0, REQS)
    return jnp.where(jnp.arange(REQS) == chosen, LMAX, drawn).astype(jnp.int32)


def draw_positions(key, part):
    step_key, slot_key = jax.random.split(key)
    step_sizes = jax.random.randint(step_key, (REQS, LMAX), 1, 3)
    chosen = jax.random.randint(slot_key, (), 0, REQS)
    slot_ids = jnp.arange(REQS)[:, None]
    row_ids = jnp.arange(LMAX)[None, :]
    step_sizes = jnp.where(slot_ids == chosen, 2, step_sizes)
    starter = (chosen + 1) % REQS
    step_sizes = jnp.where((slot_ids == starter) & (row_ids == 0), 1, step_sizes)
    return (jnp.cumsum(step_sizes, axis=1) - 1).astype(jnp.int32)


def draw_latent_cache(key, part):
    base_key = jax.random.fold_in(key, 0)
    base = jax.random.normal(base_key, (REQS, LMAX, DL), jnp.float32)
    return base.astype(jnp.bfloat16)


def plant(values, rng, smallest, top_value):
    dims = values.shape
    place = [jax.random.randint(jax.random.fold_in(rng, axis), (), 0, dims[axis]) for axis in range(len(dims))]
    values = values.at[tuple(place)].set(smallest)
    longest = dims.index(max(dims))
    place[longest] = (place[longest] + 1) % dims[longest]
    return values.at[tuple(place)].set(top_value)


def block_levels(rng, extent, pieces, low, top_value):
    def one(axis_at, shards_of):
        heights = jax.random.uniform(jax.random.fold_in(jax.random.fold_in(rng, 6), axis_at), (shards_of,), jnp.float32, low / len(pieces), top_value / len(pieces))
        return jnp.repeat(jnp.exp(heights), extent[axis_at] // shards_of).reshape((-1,) + (1,) * (len(extent) - axis_at - 1))

    loudness = one(*pieces[0])
    for cut in pieces[1:]:
        loudness = loudness * one(*cut)
    return loudness


def bell_draw(own_key, extent, deviation, reach, cuts=(), kind=jnp.bfloat16):
    values = jax.random.normal(own_key, extent, jnp.float32) * deviation
    if len(cuts) > 0:
        values = block_levels(own_key, extent, cuts, -0.22, 0.18) * values
    return jnp.clip(values, min=-reach, max=reach).astype(kind)


def setup_inputs(seed: int = 0) -> dict:
    arg_keys = jax.random.split(jax.random.key(seed), 13)
    return {
        "q_nope": bell_draw(arg_keys[0], (STEPS, REQS, H, DN), 2.5, 16.0, ((2, 4),)),
        "q_rope": bell_draw(arg_keys[1], (STEPS, REQS, H, DR), 2.5, 16.0, ((2, 4),)),
        "w_uk": bell_draw(arg_keys[2], (H, DN, DL), DN ** -0.5, 0.5, ((0, 4),)),
        "w_uv": bell_draw(arg_keys[3], (H, DL, DV), DL ** -0.5, 0.25, ((0, 4),)),
        "latent_cache": draw_latent_cache(jax.random.fold_in(arg_keys[12], 71), 0),
        "rope_cache": bell_draw(arg_keys[5], (REQS, LMAX, DR), 1.0, 6.0, ((0, 4), (1, 8))),
        "positions": draw_positions(jax.random.fold_in(arg_keys[12], 71), 0),
        "new_latent": bell_draw(arg_keys[7], (STEPS, REQS, DL), 2.0, 12.0),
        "new_rope": bell_draw(arg_keys[8], (STEPS, REQS, DR), 1.0, 6.0),
        "new_pos": plant(jax.random.randint(arg_keys[9], (REQS,), 2 * LMAX, 2 * LMAX + 4096), jax.random.fold_in(arg_keys[9], 1), 2 * LMAX, (2 * LMAX + 4096) - 1).astype(jnp.int32),
        "lengths": draw_lengths(jax.random.fold_in(arg_keys[12], 71), 0),
        "assignment": jax.random.permutation(arg_keys[11], REQS).astype(jnp.int32),
    }


def rotate(values, position):
    half_width = values.shape[-1] // 2
    frequency = jnp.exp(jnp.arange(half_width, dtype=jnp.float32) * (-2.0 * math.log(10000.0) / values.shape[-1]))
    angles = position.astype(jnp.float32)[..., None] * frequency
    cosine = jnp.cos(angles)
    sine_part = jnp.sin(angles)
    former = values[..., :half_width]
    latter = values[..., half_width:]
    return jnp.concatenate([former * cosine - latter * sine_part, latter * cosine + former * sine_part], axis=-1)

def reference(q_nope, q_rope, w_uk, w_uv, latent_cache, rope_cache, positions, new_latent, new_rope, new_pos, lengths, assignment):
    score_scale = 1.0 / math.sqrt(DN + DR)
    q_latent = jnp.einsum('srhn,hnl->srhl', q_nope.astype(jnp.float32), w_uk.astype(jnp.float32)).astype(jnp.bfloat16)
    step_ids = jnp.arange(STEPS, dtype=jnp.int32)
    query_pos = new_pos[None, :] + step_ids[:, None]
    q_rotated = rotate(q_rope.astype(jnp.float32), query_pos[:, :, None]).astype(jnp.bfloat16)
    new_keys = rotate(new_rope.astype(jnp.float32), query_pos).astype(jnp.bfloat16)
    row_ids = jnp.arange(LMAX, dtype=jnp.int32)
    step_of_row = jnp.repeat(step_ids, H)
    new_valid = step_ids[None, :] <= step_of_row[:, None]

    def attend_slot(slot_index):
        request = assignment[slot_index]
        lat_query = q_latent[:, request].reshape(STEPS * H, DL)
        rope_query = q_rotated[:, request].reshape(STEPS * H, DR)
        cached = latent_cache[slot_index]
        rotated_keys = rotate(rope_cache[slot_index].astype(jnp.float32), positions[slot_index]).astype(jnp.bfloat16)
        scores = (jnp.dot(lat_query, cached.T, preferred_element_type=jnp.float32) + jnp.dot(rope_query, rotated_keys.T, preferred_element_type=jnp.float32)) * score_scale
        valid_rows = (row_ids < lengths[request])[None, :]
        new_latents = new_latent[:, request]
        new_scores = (jnp.dot(lat_query, new_latents.T, preferred_element_type=jnp.float32) + jnp.dot(rope_query, new_keys[:, request].T, preferred_element_type=jnp.float32)) * score_scale
        row_top = jnp.maximum(lax.optimization_barrier(jnp.max(jnp.where(valid_rows, scores, -1e+30), axis=1)), lax.optimization_barrier(jnp.max(jnp.where(new_valid, new_scores, -1e+30), axis=1)))
        cache_weights = jnp.where(valid_rows, jnp.exp(scores - row_top[:, None]), 0.0)
        new_weights = jnp.where(new_valid, jnp.exp(new_scores - row_top[:, None]), 0.0)
        totals = lax.optimization_barrier(jnp.sum(cache_weights, axis=1)) + lax.optimization_barrier(jnp.sum(new_weights, axis=1))
        output_sum = jnp.dot(cache_weights.astype(jnp.bfloat16), cached, preferred_element_type=jnp.float32) + jnp.dot(new_weights.astype(jnp.bfloat16), new_latents, preferred_element_type=jnp.float32)
        return (output_sum / totals[:, None]).astype(jnp.bfloat16).reshape(STEPS, H, DL)
    by_slot = lax.map(attend_slot, jnp.arange(REQS, dtype=jnp.int32))
    by_request = jnp.zeros_like(by_slot).at[assignment].set(by_slot)
    by_request = lax.optimization_barrier(by_request)
    mixed = jnp.einsum('rshl,hlv->srhv', by_request.astype(jnp.float32), w_uv.astype(jnp.float32))
    return mixed.astype(jnp.bfloat16)
```

```python
import functools
import math

import jax
import jax.numpy as jnp
import numpy as np
from jax import lax
from jax.experimental import pallas as pl
from jax.experimental.pallas import tpu as pltpu
from jax.sharding import Mesh
from jax.sharding import PartitionSpec as P

DR = 64
DN = 128
LANES = 128
LOW = -1e30
EXPO = math.log2(math.e) / math.sqrt(DN + DR)
BF = jnp.bfloat16
F32 = jnp.float32
VMEM = pl.BlockSpec(memory_space=pltpu.VMEM)
SMEM = pl.BlockSpec(memory_space=pltpu.SMEM)
ANY = pl.BlockSpec(memory_space=pl.ANY)


def turn_rates(width):
    half = width // 2
    slope = np.float32(-2.0 * math.log(10000.0) / width)
    frequency = np.exp(np.arange(half, dtype=np.float32) * slope).astype(np.float64)
    return np.round(frequency / (2.0 * math.pi) * 2.0**32).astype(np.int64).astype(np.int32)


def sin_cos(phase):
    x = phase.astype(F32) * np.float32(math.pi * 2.0**-32)
    z = x * x
    s = np.float32(2.7525562e-06)
    for c in (-0.00019840874, 0.0083333310, -0.16666667, 1.0):
        s = s * z + np.float32(c)
    s = s * x
    c = np.float32(-2.6051615e-07)
    for k in (2.4760495e-05, -0.0013888378, 0.041666638, -0.5, 1.0):
        c = c * z + np.float32(k)
    return 2.0 * s * c, 1.0 - 2.0 * s * s


def split3(x):
    a = x.astype(BF)
    r = x - a.astype(F32)
    b = r.astype(BF)
    return a.astype(F32), b.astype(F32), r - b.astype(F32)


def stat_lanes(rows, values):
    lane = lax.broadcasted_iota(jnp.int32, (rows, LANES), 1)
    tile = jnp.zeros((rows, LANES), F32)
    for i, v in enumerate(values):
        tile = jnp.where(lane == i, v, tile)
    return tile


def absorb_kernel(dims, assign, new_pos, qn, qr, rate, w_hbm, *rest):
    R, J, T, HC, DL = dims
    outs, wbuf, sem = rest[:R], rest[R], rest[R + 1]
    g, c = lax.axis_index("req"), lax.axis_index("core")
    piece = HC // 4
    copies = []
    for i in range(4):
        copies.append(
            pltpu.make_async_copy(
                w_hbm.at[pl.ds(c * HC + i * piece, piece)],
                wbuf.at[pl.ds(i * piece, piece)],
                sem.at[i],
            )
        )
        copies[-1].start()
    tokens = [(k, j, t) for k in range(R) for j in range(J) for t in range(T)]
    who = [assign[(g ^ k) * J + j] for k, j, t in tokens]
    half = pl.ds(pl.multiple_of(c * HC, HC), HC)
    x = jnp.stack([qn[t, who[i], half, :].astype(F32) for i, (k, j, t) in enumerate(tokens)])
    x = jnp.swapaxes(x, 0, 1).astype(BF)
    row = lax.broadcasted_iota(jnp.int32, (len(tokens), DR), 0)
    pos = jnp.zeros((len(tokens), DR), jnp.int32)
    for i, (k, j, t) in enumerate(tokens):
        pos = jnp.where(row == i, new_pos[who[i]] + t, pos)
    sine, cosine = sin_cos(pos * rate[...])
    lane = lax.broadcasted_iota(jnp.int32, (len(tokens), DR), 1)
    sine = jnp.where(lane < DR // 2, -sine, sine)
    one = (lax.broadcasted_iota(jnp.int32, (HC, LANES - DR), 1) == 0).astype(F32)
    for i, (k, j, t) in enumerate(tokens):
        v = qr[t, who[i], half, :].astype(F32)
        swapped = jnp.concatenate([v[:, DR // 2 :], v[:, : DR // 2]], axis=1)
        turned = v * cosine[i : i + 1] + swapped * sine[i : i + 1]
        outs[k][j, t, :, DL:] = jnp.concatenate([turned, one], axis=1).astype(BF)
    ys = []
    for h in range(HC):
        if h % piece == 0:
            copies[h // piece].wait()
        ys.append(jnp.dot(x[h], wbuf[h], preferred_element_type=F32))
    y = jnp.swapaxes(jnp.stack(ys), 0, 1).astype(BF)
    for i, (k, j, t) in enumerate(tokens):
        outs[k][j, t, :, :DL] = y[i]


def rope_kernel(dims, block, assign, lengths, pos, rope, rate, out):
    J, CAP = dims
    g = lax.axis_index("req")
    shard = lax.axis_index("chip") * lax.axis_size("core") + lax.axis_index("core")
    half = DR // 2
    first = shard * CAP + pl.program_id(0) * block
    where_row = first + lax.broadcasted_iota(jnp.int32, (1, block), 1)
    sub = lax.broadcasted_iota(jnp.int32, (LANES - DR, block), 0)
    for j in range(J):
        sine, cosine = sin_cos(pos[j : j + 1, :] * rate[...])
        a = rope[j, :half, :].astype(F32)
        b = rope[j, half:, :].astype(F32)
        out[j, :half, :] = (a * cosine - b * sine).astype(BF)
        out[j, half:DR, :] = (b * cosine + a * sine).astype(BF)
        bad = where_row >= lengths[assign[g * J + j]]
        out[j, DR:, :] = jnp.where((sub == 0) & bad, LOW, 0.0).astype(BF)


def attend_kernel(
    dims, B, assign, new_pos, own, other, keys, new_lat, new_rope, rate, c_hbm,
    send, keep, q, cbuf, sbuf, acc, csem,
):
    R, J, T, HC, DL, CAP = dims
    nb = CAP // B
    NQ = T * R * 2 * HC
    g, c = lax.axis_index("req"), lax.axis_index("core")
    first_shard = (lax.axis_index("chip") == 0) & (c == 0)

    def fetch(j, i):
        rows = pl.ds(i * B, B)
        return pltpu.make_async_copy(c_hbm.at[j, rows], cbuf.at[j, rows], csem.at[j, i])

    for j in range(J):
        for i in range(nb):
            fetch(j, i).start()
    for j in range(J):
        for t in range(T):
            for k in range(R):
                mine, theirs = own[k, j, t], other[k, j, t]
                base = (t * R + k) * 2 * HC
                q[j, base : base + HC, :] = jnp.where(c == 0, mine, theirs)
                q[j, base + HC : base + 2 * HC, :] = jnp.where(c == 0, theirs, mine)
    nt = (((1,), (1,)), ((), ()))

    def score(j, i):
        rows = pl.ds(i * B, B)
        return lax.dot_general(
            q[j, :, :DL], cbuf[j, rows], nt, preferred_element_type=F32
        ) + jnp.dot(q[j, :, DL:], keys[j, :, rows], preferred_element_type=F32)

    for j in range(J):
        r = assign[g * J + j]
        fetch(j, 0).wait()
        sbuf[0] = score(j, 0)
        pick = lax.broadcasted_iota(jnp.int32, new_lat.shape[1:], 0) == r
        lat = [
            jnp.sum(jnp.where(pick, new_lat[u].astype(F32), 0.0), axis=0, keepdims=True)
            for u in range(T)
        ]
        pick = lax.broadcasted_iota(jnp.int32, new_rope.shape[1:], 0) == r
        rop = [
            jnp.sum(jnp.where(pick, new_rope[u].astype(F32), 0.0), axis=0, keepdims=True)
            for u in range(T)
        ]
        lat = jnp.concatenate(lat + [jnp.zeros((LANES - T, DL), F32)], axis=0).astype(BF)
        rop = jnp.concatenate(rop + [jnp.zeros((8 - T, DR), F32)], axis=0)
        step = lax.broadcasted_iota(jnp.int32, (8, DR), 0)
        lane = lax.broadcasted_iota(jnp.int32, (8, DR), 1)
        sine, cosine = sin_cos((new_pos[r] + step) * rate[:8])
        sine = jnp.where(lane < DR // 2, -sine, sine)
        swapped = jnp.concatenate([rop[:, DR // 2 :], rop[:, : DR // 2]], axis=1)
        rop = rop * cosine + swapped * sine
        rop = jnp.concatenate([rop, jnp.zeros((8, LANES - DR), F32)], axis=1)
        rop = jnp.concatenate([rop, jnp.zeros((LANES - 8, LANES), F32)], axis=0).astype(BF)
        s = lax.dot_general(q[j, :, :DL], lat, nt, preferred_element_type=F32)
        s = s + lax.dot_general(q[j, :, DL:], rop, nt, preferred_element_type=F32)
        u = lax.broadcasted_iota(jnp.int32, (NQ, LANES), 1)
        t_of = lax.broadcasted_iota(jnp.int32, (NQ, LANES), 0) // (NQ // T)
        valid = (u <= t_of) & (u < T) & first_shard
        m = jnp.max(jnp.where(valid, s, LOW), axis=1, keepdims=True)
        p = jnp.where(valid, jnp.exp2(s * EXPO - m * EXPO), 0.0)
        l = jnp.sum(p, axis=1, keepdims=True)
        acc[...] = jnp.dot(p.astype(BF), lat, preferred_element_type=F32)
        for i in range(nb):
            if i + 1 < nb:
                fetch(j, i + 1).wait()
                sbuf[(i + 1) % 2] = score(j, i + 1)
            s = sbuf[i % 2]
            top = jnp.maximum(m, jnp.max(s, axis=1, keepdims=True))
            shrink = jnp.exp2((m - top) * EXPO)
            p = jnp.exp2(s * EXPO - top * EXPO)
            l = l * shrink + jnp.sum(p, axis=1, keepdims=True)
            acc[...] = acc[...] * shrink + jnp.dot(
                p.astype(BF), cbuf[j, pl.ds(i * B, B)], preferred_element_type=F32
            )
            m = top
        whole = stat_lanes(NQ, (m, l))
        parts = stat_lanes(NQ, split3(m) + split3(l))
        for t in range(T):
            for k in range(R):
                base = (t * R + k) * 2 * HC
                lo, hi = slice(base, base + HC), slice(base + HC, base + 2 * HC)
                keep[j, t, k, :, :DL] = jnp.where(c == 0, acc[lo], acc[hi])
                send[j, t, k, :, :DL] = jnp.where(c == 0, acc[hi], acc[lo]).astype(BF)
                keep[j, t, k, :, DL:] = jnp.where(c == 0, whole[lo], whole[hi])
                send[j, t, k, :, DL:] = jnp.where(c == 0, parts[hi], parts[lo]).astype(BF)


def pair_kernel(dims, keep, got, out):
    R, J, T, HC, HS, CH, DL = dims
    g = lax.axis_index("req")
    HB = HC // HS
    for j in range(J):
        for t in range(T):
            for k in range(R):
                a = keep[j, t, k]
                b = got[j, t, k].astype(F32)
                ma, la = a[:, DL : DL + 1], a[:, DL + 1 : DL + 2]
                mb = b[:, DL : DL + 1] + b[:, DL + 1 : DL + 2] + b[:, DL + 2 : DL + 3]
                lb = b[:, DL + 3 : DL + 4] + b[:, DL + 4 : DL + 5] + b[:, DL + 5 : DL + 6]
                m = jnp.maximum(ma, mb)
                wa, wb = jnp.exp2((ma - m) * EXPO), jnp.exp2((mb - m) * EXPO)
                o = (a[:, :DL] * wa + b[:, :DL] * wb).astype(BF)
                st = stat_lanes(HC, split3(m) + split3(la * wa + lb * wb)).astype(BF)
                for s in range(HS):
                    at = (g ^ k) * CH + (j * T + t) * HS + s
                    out[at, :, :DL] = o[s * HB : (s + 1) * HB]
                    out[at, :, DL:] = st[s * HB : (s + 1) * HB]


def value_kernel(dims, got, w_hbm, out, wbuf, sem):
    R, CH, HC, HS, HB, DL, DV, JT = dims
    c = lax.axis_index("core")
    part = lax.rem(lax.axis_index("chip"), HS)
    first = c * HC + part * HB
    fetch = pltpu.make_async_copy(w_hbm.at[pl.ds(first, HB)], wbuf, sem)
    fetch.start()
    rows = []
    for r in range(R):
        x = [got[r * CH + i].astype(F32) for i in range(CH)]
        ms = [v[:, DL : DL + 1] + v[:, DL + 1 : DL + 2] + v[:, DL + 2 : DL + 3] for v in x]
        ls = [v[:, DL + 3 : DL + 4] + v[:, DL + 4 : DL + 5] + v[:, DL + 5 : DL + 6] for v in x]
        m = functools.reduce(jnp.maximum, ms)
        ws = [jnp.exp2((v - m) * EXPO) for v in ms]
        total = sum(w * l for w, l in zip(ws, ls))
        o = sum(w * v[:, :DL] for w, v in zip(ws, x))
        rows.append((o / total).astype(BF).astype(F32))
    x = jnp.swapaxes(jnp.stack(rows), 0, 1).astype(BF)
    fetch.wait()
    ys = [jnp.dot(x[h], wbuf[h], preferred_element_type=F32) for h in range(HB)]
    out[...] = jnp.swapaxes(jnp.stack(ys), 0, 1).astype(BF)


def place_kernel(dims, assign, got, out):
    R, J, T, HC, HS, HB, CH = dims
    for chip in range(CH):
        jt, s = divmod(chip, HS)
        j, t = divmod(jt, T)
        for c in range(2):
            for r in range(R):
                out[t, assign[r * J + j], pl.ds(c * HC + s * HB, HB), :] = got[chip * 2 + c, r]


def body(
    q_nope, q_rope, w_uk, w_uv, latent_cache, rope_cache, positions,
    new_latent, new_rope, new_pos, lengths, assignment,
):
    T, REQS, HL, _ = q_nope.shape
    DL, DV = w_uk.shape[2], w_uv.shape[2]
    J, CAP = latent_cache.shape[:2]
    R, CH = lax.axis_size("req"), lax.axis_size("chip")
    HC = HL // 2
    HS = CH // (J * T)
    HB = HC // HS
    W = DL + LANES
    rates = turn_rates(DR)
    rate_row = jnp.asarray(np.tile(np.concatenate([rates, rates])[None], (R * J * T, 1)))
    rate_col = jnp.asarray(rates[:, None])
    big = pltpu.CompilerParams(vmem_limit_bytes=56 << 20)

    blocks = pl.pallas_call(
        functools.partial(absorb_kernel, (R, J, T, HC, DL)),
        out_shape=[jax.ShapeDtypeStruct((J, T, HC, W), BF)] * R,
        in_specs=[SMEM, SMEM, VMEM, VMEM, VMEM, ANY],
        out_specs=[VMEM] * R,
        scratch_shapes=[pltpu.VMEM((HC, DN, DL), BF), pltpu.SemaphoreType.DMA((4,))],
        compiler_params=big,
        name="absorb",
    )(assignment, new_pos, q_nope, q_rope, rate_row, w_uk)
    arrived = [blocks[0]] + [
        lax.ppermute(blocks[k], "req", [(i, i ^ k) for i in range(R)]) for k in range(1, R)
    ]
    own = jnp.stack(arrived)
    other = lax.ppermute(own, "core", [(0, 1), (1, 0)])

    KB = CAP // 3
    keys = pl.pallas_call(
        functools.partial(rope_kernel, (J, CAP), KB),
        out_shape=jax.ShapeDtypeStruct((J, LANES, CAP), BF),
        grid=(3,),
        in_specs=[
            SMEM,
            SMEM,
            pl.BlockSpec((J, KB), lambda i: (0, i)),
            pl.BlockSpec((J, DR, KB), lambda i: (0, 0, i)),
            pl.BlockSpec((DR // 2, 1), lambda i: (0, 0)),
        ],
        out_specs=pl.BlockSpec((J, LANES, KB), lambda i: (0, 0, i)),
        compiler_params=big,
        name="rope",
    )(assignment, lengths, positions, jnp.swapaxes(rope_cache, 1, 2), rate_col)

    B = 1024
    NQ = T * R * HL
    send, keep = pl.pallas_call(
        functools.partial(attend_kernel, (R, J, T, HC, DL, CAP), B),
        out_shape=[
            jax.ShapeDtypeStruct((J, T, R, HC, W), BF),
            jax.ShapeDtypeStruct((J, T, R, HC, W), F32),
        ],
        in_specs=[SMEM, SMEM, VMEM, VMEM, VMEM, VMEM, VMEM, VMEM, ANY],
        out_specs=[VMEM, VMEM],
        scratch_shapes=[
            pltpu.VMEM((J, NQ, W), BF),
            pltpu.VMEM((J, CAP, DL), BF),
            pltpu.VMEM((2, NQ, B), F32),
            pltpu.VMEM((NQ, DL), F32),
            pltpu.SemaphoreType.DMA((J, CAP // B)),
        ],
        compiler_params=big,
        name="attend",
    )(assignment, new_pos, own, other, keys, new_latent, new_rope, rate_row, latent_cache)
    got = lax.ppermute(send, "core", [(0, 1), (1, 0)])
    paired = pl.pallas_call(
        functools.partial(pair_kernel, (R, J, T, HC, HS, CH, DL)),
        out_shape=jax.ShapeDtypeStruct((R * CH, HB, W), BF),
        in_specs=[VMEM, VMEM],
        out_specs=VMEM,
        compiler_params=big,
        name="pair",
    )(keep, got)
    shares = lax.all_to_all(paired, ("req", "chip"), 0, 0)
    values = pl.pallas_call(
        functools.partial(value_kernel, (R, CH, HC, HS, HB, DL, DV, J * T)),
        out_shape=jax.ShapeDtypeStruct((R, HB, DV), BF),
        in_specs=[VMEM, ANY],
        out_specs=VMEM,
        scratch_shapes=[pltpu.VMEM((HB, DL, DV), BF), pltpu.SemaphoreType.DMA],
        compiler_params=big,
        name="value",
    )(shares, w_uv)
    gathered = lax.all_gather(values, ("chip", "core"))
    return pl.pallas_call(
        functools.partial(place_kernel, (R, J, T, HC, HS, HB, CH)),
        out_shape=jax.ShapeDtypeStruct((T, REQS, HL, DV), BF),
        in_specs=[SMEM, VMEM],
        out_specs=VMEM,
        compiler_params=big,
        name="place",
    )(assignment, gathered)


def solution(mesh):
    groups, shards = mesh.shape["req"], mesh.shape["seq"]
    cut = Mesh(mesh.devices.reshape(groups, shards // 2, 2), ("req", "chip", "core"))
    seq = ("chip", "core")
    in_specs = (
        P(None, None, "req", None),
        P(None, None, "req", None),
        P("req", None, None),
        P("req", None, None),
        P("req", seq, None),
        P("req", seq, None),
        P("req", seq),
        P(),
        P(),
        P(),
        P(),
        P(),
    )
    out_specs = P(None, None, "req", None)
    return jax.shard_map(body, mesh=cut, in_specs=in_specs, out_specs=out_specs, check_vma=False)
```

```python
import functools
import math

import jax
import jax.numpy as jnp
import numpy as np
from jax import lax
from jax.experimental import pallas as pl
from jax.experimental.pallas import tpu as pltpu
from jax.sharding import Mesh
from jax.sharding import PartitionSpec as P

DR = 64
DN = 128
LANES = 128
LOW = -1e30
EXPO = math.log2(math.e) / math.sqrt(DN + DR)
KEYS = 80
BF = jnp.bfloat16
F32 = jnp.float32
VMEM = pl.BlockSpec(memory_space=pltpu.VMEM)
SMEM = pl.BlockSpec(memory_space=pltpu.SMEM)
ANY = pl.BlockSpec(memory_space=pl.ANY)
HBM = pl.BlockSpec(memory_space=pltpu.HBM)


def in_hbm(x):
    return pltpu.with_memory_space_constraint(x, pltpu.HBM)


def turn_rates(width):
    half = width // 2
    slope = np.float32(-2.0 * math.log(10000.0) / width)
    frequency = np.exp(np.arange(half, dtype=np.float32) * slope).astype(np.float64)
    return np.round(frequency / (2.0 * math.pi) * 2.0**32).astype(np.int64).astype(np.int32)


def sin_cos(phase):
    x = phase.astype(F32) * np.float32(math.pi * 2.0**-32)
    z = x * x
    s = np.float32(2.7525562e-06)
    for c in (-0.00019840874, 0.0083333310, -0.16666667, 1.0):
        s = s * z + np.float32(c)
    s = s * x
    c = np.float32(-2.6051615e-07)
    for k in (2.4760495e-05, -0.0013888378, 0.041666638, -0.5, 1.0):
        c = c * z + np.float32(k)
    return 2.0 * s * c, 1.0 - 2.0 * s * s


def split3(x):
    a = x.astype(BF)
    r = x - a.astype(F32)
    b = r.astype(BF)
    return a.astype(F32), b.astype(F32), r - b.astype(F32)


def stat_lanes(rows, values):
    lane = lax.broadcasted_iota(jnp.int32, (rows, LANES), 1)
    tile = jnp.zeros((rows, LANES), F32)
    for i, v in enumerate(values):
        tile = jnp.where(lane == i, v, tile)
    return tile


def absorb_kernel(dims, assign, new_pos, qn, qr, rate, w_hbm, *rest):
    R, J, T, HC, DL = dims
    outs, wbuf, sem = rest[:R], rest[R], rest[R + 1]
    g, c = lax.axis_index("req"), lax.axis_index("core")
    piece = HC // 4
    copies = []
    for i in range(4):
        copies.append(
            pltpu.make_async_copy(
                w_hbm.at[pl.ds(c * HC + i * piece, piece)],
                wbuf.at[pl.ds(i * piece, piece)],
                sem.at[i],
            )
        )
        copies[-1].start()
    tokens = [(k, j, t) for k in range(R) for j in range(J) for t in range(T)]
    who = [assign[(g ^ k) * J + j] for k, j, t in tokens]
    half = pl.ds(pl.multiple_of(c * HC, HC), HC)
    x = jnp.stack([qn[t, who[i], half, :].astype(F32) for i, (k, j, t) in enumerate(tokens)])
    x = jnp.swapaxes(x, 0, 1).astype(BF)
    row = lax.broadcasted_iota(jnp.int32, (len(tokens), DR), 0)
    pos = jnp.zeros((len(tokens), DR), jnp.int32)
    for i, (k, j, t) in enumerate(tokens):
        pos = jnp.where(row == i, new_pos[who[i]] + t, pos)
    sine, cosine = sin_cos(pos * rate[...])
    lane = lax.broadcasted_iota(jnp.int32, (len(tokens), DR), 1)
    sine = jnp.where(lane < DR // 2, -sine, sine)
    one = (lax.broadcasted_iota(jnp.int32, (HC, LANES - DR), 1) == 0).astype(F32)
    for i, (k, j, t) in enumerate(tokens):
        v = qr[t, who[i], half, :].astype(F32)
        swapped = jnp.concatenate([v[:, DR // 2 :], v[:, : DR // 2]], axis=1)
        turned = v * cosine[i : i + 1] + swapped * sine[i : i + 1]
        outs[k][j, t, :, DL:] = jnp.concatenate([turned, one], axis=1).astype(BF)
    ys = []
    for h in range(HC):
        if h % piece == 0:
            copies[h // piece].wait()
        ys.append(jnp.dot(x[h], wbuf[h], preferred_element_type=F32))
    y = jnp.swapaxes(jnp.stack(ys), 0, 1).astype(BF)
    for i, (k, j, t) in enumerate(tokens):
        outs[k][j, t, :, :DL] = y[i]


def prepare_kernel(dims, cuts, assign, lengths, pos, rope, rate, c_hbm, out, c_out, sem):
    J, CAP = dims
    g = lax.axis_index("req")
    shard = lax.axis_index("chip") * lax.axis_size("core") + lax.axis_index("core")
    half = DR // 2
    block = CAP // cuts
    copies = []
    for j in range(J):
        for i in range(cuts):
            rows = pl.ds(i * block, block)
            copies.append(
                pltpu.make_async_copy(c_hbm.at[j, rows], c_out.at[j, rows], sem.at[j, i])
            )
            copies[-1].start()
    sub = lax.broadcasted_iota(jnp.int32, (KEYS - DR, block), 0)
    turn = rate[...]
    for j in range(J):
        end = lengths[assign[g * J + j]] - shard * CAP

        def rotate(i, carry):
            at = pl.ds(pl.multiple_of(i * block, LANES), block)
            sine, cosine = sin_cos(pos[j : j + 1, at] * turn)
            a = rope[j, :half, at].astype(F32)
            b = rope[j, half:, at].astype(F32)
            out[j, :half, at] = (a * cosine - b * sine).astype(BF)
            out[j, half:DR, at] = (b * cosine + a * sine).astype(BF)
            bad = i * block + lax.broadcasted_iota(jnp.int32, (1, block), 1) >= end
            out[j, DR:, at] = jnp.where((sub == 0) & bad, LOW, 0.0).astype(BF)
            return carry

        lax.fori_loop(0, cuts, rotate, 0)
    for copy in copies:
        copy.wait()


def attend_kernel(
    dims, B, assign, new_pos, new_lat, new_rope, rate, keys, cbuf, *rest
):
    R, J, T, HC, DL, CAP = dims
    own, other = rest[:R], rest[R : 2 * R]
    send, keep, q, sbuf, acc = rest[2 * R :]
    nb = CAP // B
    NQ = T * R * 2 * HC
    g, c = lax.axis_index("req"), lax.axis_index("core")
    first_shard = (lax.axis_index("chip") == 0) & (c == 0)

    for j in range(J):
        for t in range(T):
            for k in range(R):
                mine, theirs = own[k][j, t], other[k][j, t]
                base = (t * R + k) * 2 * HC
                q[j, base : base + HC, :] = jnp.where(c == 0, mine, theirs)
                q[j, base + HC : base + 2 * HC, :] = jnp.where(c == 0, theirs, mine)
    nt = (((1,), (1,)), ((), ()))

    def score(j, i):
        rows = pl.ds(i * B, B)
        return lax.dot_general(
            q[j, :, :DL], cbuf[j, rows], nt, preferred_element_type=F32
        ) + jnp.dot(
            q[j, :, DL : DL + KEYS], keys[j, :, rows], preferred_element_type=F32
        )

    for j in range(J):
        r = assign[g * J + j]
        sbuf[0] = score(j, 0)
        pick = lax.broadcasted_iota(jnp.int32, new_lat.shape[1:], 0) == r
        lat = [
            jnp.sum(jnp.where(pick, new_lat[u].astype(F32), 0.0), axis=0, keepdims=True)
            for u in range(T)
        ]
        pick = lax.broadcasted_iota(jnp.int32, new_rope.shape[1:], 0) == r
        rop = [
            jnp.sum(jnp.where(pick, new_rope[u].astype(F32), 0.0), axis=0, keepdims=True)
            for u in range(T)
        ]
        lat = jnp.concatenate(lat + [jnp.zeros((LANES - T, DL), F32)], axis=0).astype(BF)
        rop = jnp.concatenate(rop + [jnp.zeros((8 - T, DR), F32)], axis=0)
        step = lax.broadcasted_iota(jnp.int32, (8, DR), 0)
        lane = lax.broadcasted_iota(jnp.int32, (8, DR), 1)
        sine, cosine = sin_cos((new_pos[r] + step) * rate[:8])
        sine = jnp.where(lane < DR // 2, -sine, sine)
        swapped = jnp.concatenate([rop[:, DR // 2 :], rop[:, : DR // 2]], axis=1)
        rop = rop * cosine + swapped * sine
        rop = jnp.concatenate([rop, jnp.zeros((8, LANES - DR), F32)], axis=1)
        rop = jnp.concatenate([rop, jnp.zeros((LANES - 8, LANES), F32)], axis=0).astype(BF)
        s = lax.dot_general(q[j, :, :DL], lat, nt, preferred_element_type=F32)
        s = s + lax.dot_general(q[j, :, DL:], rop, nt, preferred_element_type=F32)
        u = lax.broadcasted_iota(jnp.int32, (NQ, LANES), 1)
        t_of = lax.broadcasted_iota(jnp.int32, (NQ, LANES), 0) // (NQ // T)
        valid = (u <= t_of) & (u < T) & first_shard
        m = jnp.max(jnp.where(valid, s, LOW), axis=1, keepdims=True)
        p = jnp.where(valid, jnp.exp2(s * EXPO - m * EXPO), 0.0)
        l = jnp.sum(p, axis=1, keepdims=True)
        acc[...] = jnp.dot(p.astype(BF), lat, preferred_element_type=F32)
        for i in range(nb):
            if i + 1 < nb:
                sbuf[(i + 1) % 2] = score(j, i + 1)
            s = sbuf[i % 2]
            top = jnp.maximum(m, jnp.max(s, axis=1, keepdims=True))
            shrink = jnp.exp2((m - top) * EXPO)
            p = jnp.exp2(s * EXPO - top * EXPO)
            l = l * shrink + jnp.sum(p, axis=1, keepdims=True)
            acc[...] = acc[...] * shrink + jnp.dot(
                p.astype(BF), cbuf[j, pl.ds(i * B, B)], preferred_element_type=F32
            )
            m = top
        whole = stat_lanes(NQ, (m, l))
        parts = stat_lanes(NQ, split3(m) + split3(l))
        for t in range(T):
            for k in range(R):
                base = (t * R + k) * 2 * HC
                lo, hi = slice(base, base + HC), slice(base + HC, base + 2 * HC)
                keep[j, t, k, :, :DL] = jnp.where(c == 0, acc[lo], acc[hi])
                send[j, t, k, :, :DL] = jnp.where(c == 0, acc[hi], acc[lo]).astype(BF)
                keep[j, t, k, :, DL:] = jnp.where(c == 0, whole[lo], whole[hi])
                send[j, t, k, :, DL:] = jnp.where(c == 0, parts[hi], parts[lo]).astype(BF)


def stats_of(x, DL):
    m = x[:, DL : DL + 1] + x[:, DL + 1 : DL + 2] + x[:, DL + 2 : DL + 3]
    return m, x[:, DL + 3 : DL + 4] + x[:, DL + 4 : DL + 5] + x[:, DL + 5 : DL + 6]


def pair_kernel(dims, keep, got, out):
    R, J, T, HC, HS, CH, DL = dims
    g = lax.axis_index("req")
    HB = HC // HS
    for j in range(J):
        for t in range(T):
            a = jnp.concatenate([keep[j, t, k] for k in range(R)], axis=0)
            b = jnp.concatenate([got[j, t, k] for k in range(R)], axis=0).astype(F32)
            ma, la = a[:, DL : DL + 1], a[:, DL + 1 : DL + 2]
            mb, lb = stats_of(b[:, :], DL)
            m = jnp.maximum(ma, mb)
            wa, wb = jnp.exp2((ma - m) * EXPO), jnp.exp2((mb - m) * EXPO)
            o = (a[:, :DL] * wa + b[:, :DL] * wb).astype(BF)
            st = stat_lanes(R * HC, split3(m) + split3(la * wa + lb * wb)).astype(BF)
            for k in range(R):
                for s in range(HS):
                    at = (g ^ k) * CH + (j * T + t) * HS + s
                    rows = slice(k * HC + s * HB, k * HC + (s + 1) * HB)
                    out[at, :, :DL] = o[rows]
                    out[at, :, DL:] = st[rows]


def value_kernel(dims, got, w, out):
    R, CH, HC, HS, HB, DL, DV, JT = dims
    c = lax.axis_index("core")
    part = lax.rem(lax.axis_index("chip"), HS)
    first = c * HC + part * HB
    x = [
        jnp.concatenate([got[r * CH + i] for r in range(R)], axis=0).astype(F32) for i in range(CH)
    ]
    ms, ls = zip(*[stats_of(v, DL) for v in x])
    m = functools.reduce(jnp.maximum, ms)
    ws = [jnp.exp2((v - m) * EXPO) for v in ms]
    total = sum(w_ * l for w_, l in zip(ws, ls))
    o = sum(w_ * v[:, :DL] for w_, v in zip(ws, x)) / total
    o = o.astype(BF).astype(F32).reshape(R, HB, DL)
    x = jnp.swapaxes(o, 0, 1).astype(BF)
    ys = [jnp.dot(x[h], w[first + h], preferred_element_type=F32) for h in range(HB)]
    out[...] = jnp.swapaxes(jnp.stack(ys), 0, 1).astype(BF)


def place_kernel(dims, assign, got, out):
    R, J, T, HC, HS, HB, CH = dims
    for chip in range(CH):
        jt, s = divmod(chip, HS)
        j, t = divmod(jt, T)
        for c in range(2):
            for r in range(R):
                out[t, assign[r * J + j], pl.ds(c * HC + s * HB, HB), :] = got[chip * 2 + c, r]


def body(
    q_nope, q_rope, w_uk, w_uv, latent_cache, rope_cache, positions,
    new_latent, new_rope, new_pos, lengths, assignment,
):
    T, REQS, HL, _ = q_nope.shape
    DL, DV = w_uk.shape[2], w_uv.shape[2]
    J, CAP = latent_cache.shape[:2]
    R, CH = lax.axis_size("req"), lax.axis_size("chip")
    HC = HL // 2
    HS = CH // (J * T)
    HB = HC // HS
    W = DL + LANES
    rates = turn_rates(DR)
    rate_row = jnp.asarray(np.tile(np.concatenate([rates, rates])[None], (R * J * T, 1)))
    rate_col = jnp.asarray(rates[:, None])
    assignment, new_pos, lengths = in_hbm(assignment), in_hbm(new_pos), in_hbm(lengths)
    big = pltpu.CompilerParams(vmem_limit_bytes=8 << 20)

    blocks = pl.pallas_call(
        functools.partial(absorb_kernel, (R, J, T, HC, DL)),
        out_shape=[jax.ShapeDtypeStruct((J, T, HC, W), BF)] * R,
        in_specs=[SMEM, SMEM, VMEM, VMEM, VMEM, HBM],
        out_specs=[VMEM] * R,
        scratch_shapes=[pltpu.VMEM((HC, DN, DL), BF), pltpu.SemaphoreType.DMA((4,))],
        compiler_params=big,
        name="absorb",
    )(assignment, new_pos, in_hbm(q_nope), in_hbm(q_rope), in_hbm(rate_row), in_hbm(w_uk))
    arrived = [blocks[0]] + [
        lax.ppermute(blocks[k], "req", [(i, i ^ k) for i in range(R)]) for k in range(1, R)
    ]
    cuts = CAP // 512
    keys, cached = pl.pallas_call(
        functools.partial(prepare_kernel, (J, CAP), cuts),
        out_shape=[
            jax.ShapeDtypeStruct((J, KEYS, CAP), BF),
            jax.ShapeDtypeStruct((J, CAP, DL), BF),
        ],
        in_specs=[SMEM, SMEM, VMEM, VMEM, VMEM, HBM],
        out_specs=[VMEM, VMEM],
        scratch_shapes=[pltpu.SemaphoreType.DMA((J, cuts))],
        compiler_params=pltpu.CompilerParams(vmem_limit_bytes=8 << 20),
        cost_estimate=pl.CostEstimate(
            flops=0, bytes_accessed=4 * J * CAP * DL, transcendentals=0
        ),
        name="prepare",
    )(assignment, lengths, positions, jnp.swapaxes(rope_cache, 1, 2), rate_col, in_hbm(latent_cache))

    own, keys, cached = lax.optimization_barrier((arrived, keys, cached))
    other = [lax.ppermute(v, "core", [(0, 1), (1, 0)]) for v in own]

    B = 1024
    NQ = T * R * HL
    send, keep = pl.pallas_call(
        functools.partial(attend_kernel, (R, J, T, HC, DL, CAP), B),
        out_shape=[
            jax.ShapeDtypeStruct((J, T, R, HC, W), BF),
            jax.ShapeDtypeStruct((J, T, R, HC, W), F32),
        ],
        in_specs=[SMEM, SMEM] + [VMEM] * (5 + 2 * R),
        out_specs=[VMEM, VMEM],
        scratch_shapes=[
            pltpu.VMEM((J, NQ, W), BF),
            pltpu.VMEM((2, NQ, B), F32),
            pltpu.VMEM((NQ, DL), F32),
        ],
        compiler_params=pltpu.CompilerParams(vmem_limit_bytes=16 << 20),
        name="attend",
    )(assignment, new_pos, new_latent, new_rope, rate_row, keys, cached, *own, *other)
    got = lax.ppermute(send, "core", [(0, 1), (1, 0)])
    paired = pl.pallas_call(
        functools.partial(pair_kernel, (R, J, T, HC, HS, CH, DL)),
        out_shape=jax.ShapeDtypeStruct((R * CH, HB, W), BF),
        in_specs=[VMEM, VMEM],
        out_specs=VMEM,
        compiler_params=big,
        name="pair",
    )(keep, got)
    shares = lax.all_to_all(paired, ("req", "chip"), 0, 0)
    values = pl.pallas_call(
        functools.partial(value_kernel, (R, CH, HC, HS, HB, DL, DV, J * T)),
        out_shape=jax.ShapeDtypeStruct((R, HB, DV), BF),
        in_specs=[VMEM, VMEM],
        out_specs=VMEM,
        compiler_params=big,
        name="value",
    )(shares, w_uv)
    gathered = lax.all_gather(values, ("chip", "core"))
    return pl.pallas_call(
        functools.partial(place_kernel, (R, J, T, HC, HS, HB, CH)),
        out_shape=jax.ShapeDtypeStruct((T, REQS, HL, DV), BF),
        in_specs=[SMEM, VMEM],
        out_specs=VMEM,
        compiler_params=big,
        name="place",
    )(assignment, gathered)


def solution(mesh):
    groups, shards = mesh.shape["req"], mesh.shape["seq"]
    cut = Mesh(mesh.devices.reshape(groups, shards // 2, 2), ("req", "chip", "core"))
    seq = ("chip", "core")
    in_specs = (
        P(None, None, "req", None),
        P(None, None, "req", None),
        P("req", None, None),
        P("req", None, None),
        P("req", seq, None),
        P("req", seq, None),
        P("req", seq),
        P(),
        P(),
        P(),
        P(),
        P(),
    )
    out_specs = P(None, None, "req", None)
    return jax.shard_map(body, mesh=cut, in_specs=in_specs, out_specs=out_specs, check_vma=False)
```

```python
import functools
import math

import jax
import jax.numpy as jnp
import numpy as np
from jax import lax
from jax.experimental import pallas as pl
from jax.experimental.pallas import tpu as pltpu
from jax.sharding import Mesh
from jax.sharding import PartitionSpec as P

DR = 64
DN = 128
LANES = 128
LOW = -1e30
EXPO = math.log2(math.e) / math.sqrt(DN + DR)
KEYS = 80
BF = jnp.bfloat16
F32 = jnp.float32
VMEM = pl.BlockSpec(memory_space=pltpu.VMEM)
SMEM = pl.BlockSpec(memory_space=pltpu.SMEM)
ANY = pl.BlockSpec(memory_space=pl.ANY)
HBM = pl.BlockSpec(memory_space=pltpu.HBM)


def in_hbm(x):
    return pltpu.with_memory_space_constraint(x, pltpu.HBM)


def hop(x, axis, n):
    size = lax.axis_size(axis)
    return lax.ppermute(x, axis, [(i, i ^ n) for i in range(size)])


def hops(blocks, axis):
    return [hop(blocks[k], axis, k) for k in reversed(range(1, len(blocks)))]


def turn_rates(width):
    half = width // 2
    slope = np.float32(-2.0 * math.log(10000.0) / width)
    frequency = np.exp(np.arange(half, dtype=np.float32) * slope).astype(np.float64)
    return np.round(frequency / (2.0 * math.pi) * 2.0**32).astype(np.int64).astype(np.int32)


def sin_cos(phase):
    x = phase.astype(F32) * np.float32(math.pi * 2.0**-32)
    z = x * x
    s = np.float32(2.7525562e-06)
    for c in (-0.00019840874, 0.0083333310, -0.16666667, 1.0):
        s = s * z + np.float32(c)
    s = s * x
    c = np.float32(-2.6051615e-07)
    for k in (2.4760495e-05, -0.0013888378, 0.041666638, -0.5, 1.0):
        c = c * z + np.float32(k)
    return 2.0 * s * c, 1.0 - 2.0 * s * s


def split3(x):
    a = x.astype(BF)
    r = x - a.astype(F32)
    b = r.astype(BF)
    return a.astype(F32), b.astype(F32), r - b.astype(F32)


def stat_lanes(rows, values):
    lane = lax.broadcasted_iota(jnp.int32, (rows, LANES), 1)
    tile = jnp.zeros((rows, LANES), F32)
    for i, v in enumerate(values):
        tile = jnp.where(lane == i, v, tile)
    return tile


def absorb_kernel(dims, assign, new_pos, qn, qr, rate, w_hbm, *rest):
    R, J, T, HC, DL = dims
    outs, wbuf, sem = rest[:R], rest[R], rest[R + 1]
    g, c = lax.axis_index("req"), lax.axis_index("core")
    piece = HC // 4
    copies = []
    for i in range(4):
        copies.append(
            pltpu.make_async_copy(
                w_hbm.at[pl.ds(c * HC + i * piece, piece)],
                wbuf.at[pl.ds(i * piece, piece)],
                sem.at[i],
            )
        )
        copies[-1].start()
    tokens = [(k, j, t) for k in range(R) for j in range(J) for t in range(T)]
    who = [assign[(g ^ k) * J + j] for k, j, t in tokens]
    half = pl.ds(pl.multiple_of(c * HC, HC), HC)
    x = jnp.stack([qn[t, who[i], half, :].astype(F32) for i, (k, j, t) in enumerate(tokens)])
    x = jnp.swapaxes(x, 0, 1).astype(BF)
    row = lax.broadcasted_iota(jnp.int32, (len(tokens), DR), 0)
    pos = jnp.zeros((len(tokens), DR), jnp.int32)
    for i, (k, j, t) in enumerate(tokens):
        pos = jnp.where(row == i, new_pos[who[i]] + t, pos)
    sine, cosine = sin_cos(pos * rate[...])
    lane = lax.broadcasted_iota(jnp.int32, (len(tokens), DR), 1)
    sine = jnp.where(lane < DR // 2, -sine, sine)
    one = (lax.broadcasted_iota(jnp.int32, (HC, LANES - DR), 1) == 0).astype(F32)
    for i, (k, j, t) in enumerate(tokens):
        v = qr[t, who[i], half, :].astype(F32)
        swapped = jnp.concatenate([v[:, DR // 2 :], v[:, : DR // 2]], axis=1)
        turned = v * cosine[i : i + 1] + swapped * sine[i : i + 1]
        outs[k][j, t, :, DL:] = jnp.concatenate([turned, one], axis=1).astype(BF)
    ys = []
    for h in range(HC):
        if h % piece == 0:
            copies[h // piece].wait()
        ys.append(jnp.dot(x[h], wbuf[h], preferred_element_type=F32))
    y = jnp.swapaxes(jnp.stack(ys), 0, 1).astype(BF)
    for i, (k, j, t) in enumerate(tokens):
        outs[k][j, t, :, :DL] = y[i]


def prepare_kernel(dims, cuts, assign, lengths, pos, rope, rate, c_hbm, out, c_out, sem):
    J, CAP = dims
    g = lax.axis_index("req")
    shard = lax.axis_index("chip") * lax.axis_size("core") + lax.axis_index("core")
    half = DR // 2
    block = CAP // cuts
    copies = []
    for j in range(J):
        for i in range(cuts):
            rows = pl.ds(i * block, block)
            copies.append(
                pltpu.make_async_copy(c_hbm.at[j, rows], c_out.at[j, rows], sem.at[j, i])
            )
            copies[-1].start()
    sub = lax.broadcasted_iota(jnp.int32, (KEYS - DR, block), 0)
    turn = rate[...]
    for j in range(J):
        end = lengths[assign[g * J + j]] - shard * CAP

        def rotate(i, carry):
            at = pl.ds(pl.multiple_of(i * block, LANES), block)
            sine, cosine = sin_cos(pos[j : j + 1, at] * turn)
            a = rope[j, :half, at].astype(F32)
            b = rope[j, half:, at].astype(F32)
            out[j, :half, at] = (a * cosine - b * sine).astype(BF)
            out[j, half:DR, at] = (b * cosine + a * sine).astype(BF)
            bad = i * block + lax.broadcasted_iota(jnp.int32, (1, block), 1) >= end
            out[j, DR:, at] = jnp.where((sub == 0) & bad, LOW, 0.0).astype(BF)
            return carry

        lax.fori_loop(0, cuts, rotate, 0)
    for copy in copies:
        copy.wait()


def attend_kernel(
    dims, B, assign, new_pos, new_lat, new_rope, rate, keys, cbuf, *rest
):
    R, J, T, HC, DL, CAP = dims
    own, other = rest[:R][::-1], rest[R : 2 * R][::-1]
    send, keep, q, sbuf, acc = rest[2 * R :]
    nb = CAP // B
    NQ = T * R * 2 * HC
    g, c = lax.axis_index("req"), lax.axis_index("core")
    first_shard = (lax.axis_index("chip") == 0) & (c == 0)

    for j in range(J):
        for t in range(T):
            for k in range(R):
                mine, theirs = own[k][j, t], other[k][j, t]
                base = (t * R + k) * 2 * HC
                q[j, base : base + HC, :] = jnp.where(c == 0, mine, theirs)
                q[j, base + HC : base + 2 * HC, :] = jnp.where(c == 0, theirs, mine)
    nt = (((1,), (1,)), ((), ()))

    def score(j, i):
        rows = pl.ds(i * B, B)
        return lax.dot_general(
            q[j, :, :DL], cbuf[j, rows], nt, preferred_element_type=F32
        ) + jnp.dot(
            q[j, :, DL : DL + KEYS], keys[j, :, rows], preferred_element_type=F32
        )

    sbuf[0] = score(0, 0)
    for j in range(J):
        r = assign[g * J + j]
        pick = lax.broadcasted_iota(jnp.int32, new_lat.shape[1:], 0) == r
        lat = [
            jnp.sum(jnp.where(pick, new_lat[u].astype(F32), 0.0), axis=0, keepdims=True)
            for u in range(T)
        ]
        pick = lax.broadcasted_iota(jnp.int32, new_rope.shape[1:], 0) == r
        rop = [
            jnp.sum(jnp.where(pick, new_rope[u].astype(F32), 0.0), axis=0, keepdims=True)
            for u in range(T)
        ]
        lat = jnp.concatenate(lat + [jnp.zeros((LANES - T, DL), F32)], axis=0).astype(BF)
        rop = jnp.concatenate(rop + [jnp.zeros((8 - T, DR), F32)], axis=0)
        step = lax.broadcasted_iota(jnp.int32, (8, DR), 0)
        lane = lax.broadcasted_iota(jnp.int32, (8, DR), 1)
        sine, cosine = sin_cos((new_pos[r] + step) * rate[:8])
        sine = jnp.where(lane < DR // 2, -sine, sine)
        swapped = jnp.concatenate([rop[:, DR // 2 :], rop[:, : DR // 2]], axis=1)
        rop = rop * cosine + swapped * sine
        rop = jnp.concatenate([rop, jnp.zeros((8, LANES - DR), F32)], axis=1)
        rop = jnp.concatenate([rop, jnp.zeros((LANES - 8, LANES), F32)], axis=0).astype(BF)
        s = lax.dot_general(q[j, :, :DL], lat, nt, preferred_element_type=F32)
        s = s + lax.dot_general(q[j, :, DL:], rop, nt, preferred_element_type=F32)
        u = lax.broadcasted_iota(jnp.int32, (NQ, LANES), 1)
        t_of = lax.broadcasted_iota(jnp.int32, (NQ, LANES), 0) // (NQ // T)
        valid = (u <= t_of) & (u < T) & first_shard
        m = jnp.max(jnp.where(valid, s, LOW), axis=1, keepdims=True)
        p = jnp.where(valid, jnp.exp2(s * EXPO - m * EXPO), 0.0)
        l = jnp.sum(p, axis=1, keepdims=True)
        acc[j] = jnp.dot(p.astype(BF), lat, preferred_element_type=F32)
        for i in range(nb):
            at = j * nb + i
            if at + 1 < J * nb:
                sbuf[(at + 1) % 2] = score((at + 1) // nb, (at + 1) % nb)
            s = sbuf[at % 2]
            top = jnp.maximum(m, jnp.max(s, axis=1, keepdims=True))
            shrink = jnp.exp2((m - top) * EXPO)
            p = jnp.exp2(s * EXPO - top * EXPO)
            l = l * shrink + jnp.sum(p, axis=1, keepdims=True)
            acc[j] = acc[j] * shrink + jnp.dot(
                p.astype(BF), cbuf[j, pl.ds(i * B, B)], preferred_element_type=F32
            )
            m = top
        whole = stat_lanes(NQ, (m, l))
        parts = stat_lanes(NQ, split3(m) + split3(l))
        for t in range(T):
            for k in range(R):
                base = (t * R + k) * 2 * HC
                lo, hi = slice(base, base + HC), slice(base + HC, base + 2 * HC)
                keep[j, t, k, :, :DL] = jnp.where(c == 0, acc[j, lo], acc[j, hi])
                send[j, t, k, :, :DL] = jnp.where(c == 0, acc[j, hi], acc[j, lo]).astype(BF)
                keep[j, t, k, :, DL:] = jnp.where(c == 0, whole[lo], whole[hi])
                send[j, t, k, :, DL:] = jnp.where(c == 0, parts[hi], parts[lo]).astype(BF)


def stats_of(x, DL):
    m = x[:, DL : DL + 1] + x[:, DL + 1 : DL + 2] + x[:, DL + 2 : DL + 3]
    return m, x[:, DL + 3 : DL + 4] + x[:, DL + 4 : DL + 5] + x[:, DL + 5 : DL + 6]


def pair_kernel(dims, keep, got, *outs):
    R, J, T, HC, HS, CH, DL = dims
    HB = HC // HS
    chip = lax.axis_index("chip")
    for n in range(CH):
        token = (chip ^ n) // HS
        j, t = token // T, lax.rem(token, T)
        part = lax.rem(chip ^ n, HS)

        def chosen(ref, k):
            v = ref[j, t, k].astype(F32)
            rows = v[:HB]
            for s in range(1, HS):
                rows = jnp.where(part == s, v[s * HB : (s + 1) * HB], rows)
            return rows

        a = jnp.concatenate([chosen(keep, k) for k in range(R)], axis=0)
        b = jnp.concatenate([chosen(got, k) for k in range(R)], axis=0)
        ma, la = a[:, DL : DL + 1], a[:, DL + 1 : DL + 2]
        mb, lb = stats_of(b, DL)
        m = jnp.maximum(ma, mb)
        wa, wb = jnp.exp2((ma - m) * EXPO), jnp.exp2((mb - m) * EXPO)
        o = a[:, :DL] * wa + b[:, :DL] * wb
        l = la * wa + lb * wb
        outs[n][:, :DL] = o.astype(outs[n].dtype)
        tile = stat_lanes(R * HB, (m, l) if n == 0 else split3(m) + split3(l))
        outs[n][:, DL:] = tile.astype(outs[n].dtype)


def combine_kernel(dims, *rest):
    R, HB, DL = dims
    outs = rest[len(rest) - R :]
    *got, own = rest[: len(rest) - R]
    x = [own[...]] + [v[...].astype(F32) for v in got]
    ms, ls = zip(*[(x[0][:, DL : DL + 1], x[0][:, DL + 1 : DL + 2])] + [stats_of(v, DL) for v in x[1:]])
    m = functools.reduce(jnp.maximum, ms)
    ws = [jnp.exp2((v - m) * EXPO) for v in ms]
    total = sum(w_ * l for w_, l in zip(ws, ls))
    o = (sum(w_ * v[:, :DL] for w_, v in zip(ws, x)) / total).astype(BF)
    for k in range(R):
        outs[k][...] = o[k * HB : (k + 1) * HB]


def value_kernel(dims, w, *rest):
    R, HC, HS, HB = dims
    got, out = rest[:R][::-1], rest[R]
    first = lax.axis_index("core") * HC + lax.rem(lax.axis_index("chip"), HS) * HB
    x = jnp.stack([v[...].astype(F32) for v in got])
    x = jnp.swapaxes(x, 0, 1).astype(BF)
    ys = [jnp.dot(x[h], w[first + h], preferred_element_type=F32) for h in range(HB)]
    out[...] = jnp.swapaxes(jnp.stack(ys), 0, 1).astype(BF)


def place_kernel(dims, assign, *rest):
    R, J, T, HC, HS, HB, CH = dims
    blocks, out = rest[: 2 * CH], rest[2 * CH]
    g, chip, c = lax.axis_index("req"), lax.axis_index("chip"), lax.axis_index("core")
    for n in range(CH):
        token = (chip ^ n) // HS
        j, t = token // T, lax.rem(token, T)
        for b in range(2):
            block = blocks[2 * (CH - 1 - n) + b]
            first = (c ^ b) * HC + lax.rem(chip ^ n, HS) * HB
            for k in range(R):
                request = assign[(g ^ k) * J + j]
                if HS == 1:
                    rows = pl.ds(pl.multiple_of(first, HB), HB)
                    out[t, request, rows, :] = block[k]
                    continue
                for at in range(0, 2 * HC, HB):

                    @pl.when(first == at)
                    def _():
                        out[t, request, at : at + HB, :] = block[k]


def body(
    q_nope, q_rope, w_uk, w_uv, latent_cache, rope_cache, positions,
    new_latent, new_rope, new_pos, lengths, assignment,
):
    T, REQS, HL, _ = q_nope.shape
    DL, DV = w_uk.shape[2], w_uv.shape[2]
    J, CAP = latent_cache.shape[:2]
    R, CH = lax.axis_size("req"), lax.axis_size("chip")
    HC = HL // 2
    HS = CH // (J * T)
    HB = HC // HS
    W = DL + LANES
    rates = turn_rates(DR)
    rate_row = jnp.asarray(np.tile(np.concatenate([rates, rates])[None], (R * J * T, 1)))
    rate_col = jnp.asarray(rates[:, None])
    assignment, new_pos, lengths = in_hbm(assignment), in_hbm(new_pos), in_hbm(lengths)
    big = pltpu.CompilerParams(vmem_limit_bytes=8 << 20)

    blocks = pl.pallas_call(
        functools.partial(absorb_kernel, (R, J, T, HC, DL)),
        out_shape=[jax.ShapeDtypeStruct((J, T, HC, W), BF)] * R,
        in_specs=[SMEM, SMEM, VMEM, VMEM, VMEM, HBM],
        out_specs=[VMEM] * R,
        scratch_shapes=[pltpu.VMEM((HC, DN, DL), BF), pltpu.SemaphoreType.DMA((4,))],
        compiler_params=big,
        name="absorb",
    )(assignment, new_pos, in_hbm(q_nope), in_hbm(q_rope), in_hbm(rate_row), in_hbm(w_uk))
    arrived = hops(blocks, "req")
    near = hop(blocks[0], "core", 1)

    cuts = CAP // 512
    keys, cached = pl.pallas_call(
        functools.partial(prepare_kernel, (J, CAP), cuts),
        out_shape=[
            jax.ShapeDtypeStruct((J, KEYS, CAP), BF),
            jax.ShapeDtypeStruct((J, CAP, DL), BF),
        ],
        in_specs=[SMEM, SMEM, VMEM, VMEM, VMEM, HBM],
        out_specs=[VMEM, VMEM],
        scratch_shapes=[pltpu.SemaphoreType.DMA((J, cuts))],
        compiler_params=pltpu.CompilerParams(vmem_limit_bytes=8 << 20),
        cost_estimate=pl.CostEstimate(
            flops=0, bytes_accessed=4 * J * CAP * DL, transcendentals=0
        ),
        name="prepare",
    )(assignment, lengths, positions, jnp.swapaxes(rope_cache, 1, 2), rate_col, in_hbm(latent_cache))

    arrived, keys, cached = lax.optimization_barrier((arrived, keys, cached))
    own = arrived + [blocks[0]]
    other = [hop(v, "core", 1) for v in arrived] + [near]

    B = 1024
    NQ = T * R * HL
    send, keep = pl.pallas_call(
        functools.partial(attend_kernel, (R, J, T, HC, DL, CAP), B),
        out_shape=[
            jax.ShapeDtypeStruct((J, T, R, HC, W), BF),
            jax.ShapeDtypeStruct((J, T, R, HC, W), F32),
        ],
        in_specs=[SMEM, SMEM] + [VMEM] * (5 + 2 * R),
        out_specs=[VMEM, VMEM],
        scratch_shapes=[
            pltpu.VMEM((J, NQ, W), BF),
            pltpu.VMEM((2, NQ, B), F32),
            pltpu.VMEM((J, NQ, DL), F32),
        ],
        compiler_params=pltpu.CompilerParams(vmem_limit_bytes=16 << 20),
        name="attend",
    )(assignment, new_pos, new_latent, new_rope, rate_row, keys, cached, *own, *other)
    got = hop(send, "core", 1)
    pieces = pl.pallas_call(
        functools.partial(pair_kernel, (R, J, T, HC, HS, CH, DL)),
        out_shape=[jax.ShapeDtypeStruct((R * HB, W), BF if n else F32) for n in range(CH)],
        in_specs=[VMEM, VMEM],
        out_specs=[VMEM] * CH,
        compiler_params=big,
        name="pair",
    )(keep, got)
    shares = hops(pieces, "chip") + [pieces[0]]
    latents = pl.pallas_call(
        functools.partial(combine_kernel, (R, HB, DL)),
        out_shape=[jax.ShapeDtypeStruct((HB, DL), BF)] * R,
        in_specs=[VMEM] * CH,
        out_specs=[VMEM] * R,
        compiler_params=big,
        name="combine",
    )(*shares)
    returned = hops(latents, "req") + [latents[0]]
    values = pl.pallas_call(
        functools.partial(value_kernel, (R, HC, HS, HB)),
        out_shape=jax.ShapeDtypeStruct((R, HB, DV), BF),
        in_specs=[VMEM] * (1 + R),
        out_specs=VMEM,
        compiler_params=big,
        name="value",
    )(w_uv, *returned)
    gathered = []
    for block in hops([values] * CH, "chip") + [values]:
        gathered += [block, hop(block, "core", 1)]
    return pl.pallas_call(
        functools.partial(place_kernel, (R, J, T, HC, HS, HB, CH)),
        out_shape=jax.ShapeDtypeStruct((T, REQS, HL, DV), BF),
        in_specs=[SMEM] + [VMEM] * (2 * CH),
        out_specs=VMEM,
        compiler_params=big,
        name="place",
    )(assignment, *gathered)


def solution(mesh):
    groups, shards = mesh.shape["req"], mesh.shape["seq"]
    cut = Mesh(mesh.devices.reshape(groups, shards // 2, 2), ("req", "chip", "core"))
    seq = ("chip", "core")
    in_specs = (
        P(None, None, "req", None),
        P(None, None, "req", None),
        P("req", None, None),
        P("req", None, None),
        P("req", seq, None),
        P("req", seq, None),
        P("req", seq),
        P(),
        P(),
        P(),
        P(),
        P(),
    )
    out_specs = P(None, None, "req", None)
    return jax.shard_map(body, mesh=cut, in_specs=in_specs, out_specs=out_specs, check_vma=False)
```

```python
import functools
import math

import jax
import jax.numpy as jnp
import numpy as np
from jax import lax
from jax.experimental import pallas as pl
from jax.experimental.pallas import tpu as pltpu
from jax.sharding import Mesh
from jax.sharding import PartitionSpec as P

DR = 64
DN = 128
LANES = 128
LOW = -1e30
EXPO = math.log2(math.e) / math.sqrt(DN + DR)
KEYS = 80
BF = jnp.bfloat16
F32 = jnp.float32
VMEM = pl.BlockSpec(memory_space=pltpu.VMEM)
SMEM = pl.BlockSpec(memory_space=pltpu.SMEM)
ANY = pl.BlockSpec(memory_space=pl.ANY)
HBM = pl.BlockSpec(memory_space=pltpu.HBM)


def in_hbm(x):
    return pltpu.with_memory_space_constraint(x, pltpu.HBM)


def hop(x, axis, n):
    size = lax.axis_size(axis)
    return lax.ppermute(x, axis, [(i, i ^ n) for i in range(size)])


def hops(blocks, axis):
    return [hop(blocks[k], axis, k) for k in reversed(range(1, len(blocks)))]


def turn_rates(width):
    half = width // 2
    slope = np.float32(-2.0 * math.log(10000.0) / width)
    frequency = np.exp(np.arange(half, dtype=np.float32) * slope).astype(np.float64)
    return np.round(frequency / (2.0 * math.pi) * 2.0**32).astype(np.int64).astype(np.int32)


def sin_cos(phase):
    x = phase.astype(F32) * np.float32(math.pi * 2.0**-32)
    z = x * x
    s = np.float32(2.7525562e-06)
    for c in (-0.00019840874, 0.0083333310, -0.16666667, 1.0):
        s = s * z + np.float32(c)
    s = s * x
    c = np.float32(-2.6051615e-07)
    for k in (2.4760495e-05, -0.0013888378, 0.041666638, -0.5, 1.0):
        c = c * z + np.float32(k)
    return 2.0 * s * c, 1.0 - 2.0 * s * s


def split3(x):
    a = x.astype(BF)
    r = x - a.astype(F32)
    b = r.astype(BF)
    return a.astype(F32), b.astype(F32), r - b.astype(F32)


def stat_lanes(rows, values):
    lane = lax.broadcasted_iota(jnp.int32, (rows, LANES), 1)
    tile = jnp.zeros((rows, LANES), F32)
    for i, v in enumerate(values):
        tile = jnp.where(lane == i, v, tile)
    return tile


def absorb_kernel(dims, assign, new_pos, rate, qn_hbm, qr_hbm, w_hbm, *rest):
    R, J, T, HC, DL = dims
    outs, wbuf, qn, qr, sem = rest[:R], *rest[R:]
    g, c = lax.axis_index("req"), lax.axis_index("core")
    piece = HC // 4
    inputs = [
        pltpu.make_async_copy(qn_hbm, qn, sem.at[4]),
        pltpu.make_async_copy(qr_hbm, qr, sem.at[5]),
    ]
    for copy in inputs:
        copy.start()
    copies = []
    for i in range(4):
        copies.append(
            pltpu.make_async_copy(
                w_hbm.at[pl.ds(c * HC + i * piece, piece)],
                wbuf.at[pl.ds(i * piece, piece)],
                sem.at[i],
            )
        )
        copies[-1].start()
    tokens = [(k, j, t) for k in range(R) for j in range(J) for t in range(T)]
    who = [assign[(g ^ k) * J + j] for k, j, t in tokens]
    half = pl.ds(pl.multiple_of(c * HC, HC), HC)
    row = lax.broadcasted_iota(jnp.int32, (len(tokens), DR), 0)
    pos = jnp.zeros((len(tokens), DR), jnp.int32)
    for i, (k, j, t) in enumerate(tokens):
        pos = jnp.where(row == i, new_pos[who[i]] + t, pos)
    sine, cosine = sin_cos(pos * rate[...])
    lane = lax.broadcasted_iota(jnp.int32, (len(tokens), DR), 1)
    sine = jnp.where(lane < DR // 2, -sine, sine)
    lane = lax.broadcasted_iota(jnp.int32, (HC, LANES - DR), 1)
    for copy in inputs:
        copy.wait()
    x = jnp.stack([qn[t, who[i], half, :].astype(F32) for i, (k, j, t) in enumerate(tokens)])
    x = jnp.swapaxes(x, 0, 1).astype(BF)
    for i, (k, j, t) in enumerate(tokens):
        v = qr[t, who[i], half, :].astype(F32)
        swapped = jnp.concatenate([v[:, DR // 2 :], v[:, : DR // 2]], axis=1)
        turned = v * cosine[i : i + 1] + swapped * sine[i : i + 1]
        one = ((lane == 0) | ((lane > t) & (lane < T))).astype(F32)
        outs[k][j, t, :, DL:] = jnp.concatenate([turned, one], axis=1).astype(BF)
    ys = []
    for h in range(HC):
        if h % piece == 0:
            copies[h // piece].wait()
        ys.append(jnp.dot(x[h], wbuf[h], preferred_element_type=F32))
    y = jnp.swapaxes(jnp.stack(ys), 0, 1).astype(BF)
    for i, (k, j, t) in enumerate(tokens):
        outs[k][j, t, :, :DL] = y[i]


def prepare_kernel(
    dims, cuts, assign, lengths, new_pos, new_lat, new_rope, rate_row,
    pos, rope, rate, c_hbm, out, c_out, sem,
):
    J, T, CAP, DL = dims
    g = lax.axis_index("req")
    shard = lax.axis_index("chip") * lax.axis_size("core") + lax.axis_index("core")
    half = DR // 2
    block = CAP // cuts
    copies = []
    for j in range(J):
        for i in range(cuts):
            rows = pl.ds(i * block, block)
            copies.append(
                pltpu.make_async_copy(c_hbm.at[j, rows], c_out.at[j, rows], sem.at[j, i])
            )
            copies[-1].start()
    sub = lax.broadcasted_iota(jnp.int32, (KEYS - DR, block), 0)
    turn = rate[...]
    for j in range(J):
        end = lengths[assign[g * J + j]] - shard * CAP

        def rotate(i, carry):
            at = pl.ds(pl.multiple_of(i * block, LANES), block)
            sine, cosine = sin_cos(pos[j : j + 1, at] * turn)
            a = rope[j, :half, at].astype(F32)
            b = rope[j, half:, at].astype(F32)
            out[j, :half, at] = (a * cosine - b * sine).astype(BF)
            out[j, half:DR, at] = (b * cosine + a * sine).astype(BF)
            bad = i * block + lax.broadcasted_iota(jnp.int32, (1, block), 1) >= end
            out[j, DR:, at] = jnp.where((sub == 0) & bad, LOW, 0.0).astype(BF)
            return carry

        lax.fori_loop(0, cuts, rotate, 0)
    for j in range(J):
        r = assign[g * J + j]
        pick = lax.broadcasted_iota(jnp.int32, new_lat.shape[1:], 0) == r
        lat = [
            jnp.sum(jnp.where(pick, new_lat[u].astype(F32), 0.0), axis=0, keepdims=True)
            for u in range(T)
        ]
        pick = lax.broadcasted_iota(jnp.int32, new_rope.shape[1:], 0) == r
        rop = [
            jnp.sum(jnp.where(pick, new_rope[u].astype(F32), 0.0), axis=0, keepdims=True)
            for u in range(T)
        ]
        lat = jnp.concatenate(lat + [jnp.zeros((LANES - T, DL), F32)], axis=0)
        c_out[j, CAP:, :] = lat.astype(BF)
        rop = jnp.concatenate(rop + [jnp.zeros((8 - T, DR), F32)], axis=0)
        step = lax.broadcasted_iota(jnp.int32, (8, DR), 0)
        lane = lax.broadcasted_iota(jnp.int32, (8, DR), 1)
        sine, cosine = sin_cos((new_pos[r] + step) * rate_row[:8])
        sine = jnp.where(lane < DR // 2, -sine, sine)
        swapped = jnp.concatenate([rop[:, DR // 2 :], rop[:, : DR // 2]], axis=1)
        rop = rop * cosine + swapped * sine
        rop = jnp.concatenate([rop, jnp.zeros((LANES - 8, DR), F32)], axis=0)
        u = lax.broadcasted_iota(jnp.int32, (LANES, LANES - DR), 0)
        lane = lax.broadcasted_iota(jnp.int32, (LANES, LANES - DR), 1)
        absent = (lane == 0) & ((u >= T) | (shard > 0))
        later = (lane > 0) & (lane == u) & (u < T)
        rop = jnp.concatenate([rop, jnp.where(absent | later, LOW, 0.0)], axis=1)
        out[j, :, CAP:] = jnp.transpose(rop)[:KEYS].astype(BF)
    for copy in copies:
        copy.wait()


def units(R, c):
    found = [(0, c), (R - 1, c)]
    for i in range(1, R // 2):
        found += [(2 * i - c, 0), (2 * i - c, 1)]
    return found


def attend_kernel(dims, B, keys, cbuf, *rest):
    R, J, T, HC, DL, CAP = dims
    own, other = rest[:R][::-1], rest[R : 2 * R][::-1]
    send, keep, q, sbuf, acc = rest[2 * R :]
    nb = CAP // B
    NQ = T * R * 2 * HC
    c = lax.axis_index("core")
    for j in range(J):
        for t in range(T):
            for k in range(R):
                mine, theirs = own[k][j, t], other[k][j, t]
                base = (t * R + k) * 2 * HC
                q[j, base : base + HC, :] = jnp.where(c == 0, mine, theirs)
                q[j, base + HC : base + 2 * HC, :] = jnp.where(c == 0, theirs, mine)
    nt = (((1,), (1,)), ((), ()))
    blocks = [
        (j, pl.ds(i * B, B + (LANES if i == nb - 1 else 0))) for j in range(J) for i in range(nb)
    ]

    def score(n):
        j, rows = blocks[n]
        s = lax.dot_general(q[j, :, :DL], cbuf[j, rows], nt, preferred_element_type=F32)
        s = s + jnp.dot(
            q[j, :, DL : DL + KEYS], keys[j, :, rows], preferred_element_type=F32
        )
        sbuf[n % 2, :, : rows.size] = s

    score(0)
    for n, (j, rows) in enumerate(blocks):
        if n + 1 < len(blocks):
            score(n + 1)
        s = sbuf[n % 2, :, : rows.size]
        top = jnp.max(s, axis=1, keepdims=True)
        if n % nb:
            top = jnp.maximum(m, top)
        p = jnp.exp2(s * EXPO - top * EXPO)
        part = jnp.sum(p, axis=1, keepdims=True)
        value = jnp.dot(p.astype(BF), cbuf[j, rows], preferred_element_type=F32)
        if n % nb:
            shrink = jnp.exp2((m - top) * EXPO)
            l = l * shrink + part
            acc[j] = acc[j] * shrink + value
        else:
            l = part
            acc[j] = value
        m = top
        if n % nb < nb - 1:
            continue
        whole = stat_lanes(NQ, (m, l))
        parts = stat_lanes(NQ, split3(m) + split3(l))
        for t in range(T):
            for slot in range(R):
                lo, hi = [
                    slice((t * R + k) * 2 * HC + h * HC, (t * R + k) * 2 * HC + (h + 1) * HC)
                    for k, h in (units(R, 0)[slot], units(R, 1)[slot])
                ]
                keep[j, t, slot, :, :DL] = jnp.where(c == 0, acc[j, lo], acc[j, hi])
                send[j, t, slot, :, :DL] = jnp.where(c == 0, acc[j, hi], acc[j, lo]).astype(BF)
                keep[j, t, slot, :, DL:] = jnp.where(c == 0, whole[lo], whole[hi])
                send[j, t, slot, :, DL:] = jnp.where(c == 0, parts[hi], parts[lo]).astype(BF)


def stats_of(x, DL):
    m = x[:, DL : DL + 1] + x[:, DL + 1 : DL + 2] + x[:, DL + 2 : DL + 3]
    return m, x[:, DL + 3 : DL + 4] + x[:, DL + 4 : DL + 5] + x[:, DL + 5 : DL + 6]


def pair_kernel(dims, keep, got, *outs):
    R, J, T, HC, HS, CH, DL = dims
    HB = HC // HS
    chip = lax.axis_index("chip")
    for n in range(CH):
        token = (chip ^ n) // HS
        j, t = token // T, lax.rem(token, T)
        part = lax.rem(chip ^ n, HS)

        def chosen(ref, k):
            v = ref[j, t, k].astype(F32)
            rows = v[:HB]
            for s in range(1, HS):
                rows = jnp.where(part == s, v[s * HB : (s + 1) * HB], rows)
            return rows

        a = jnp.concatenate([chosen(keep, k) for k in range(R)], axis=0)
        b = jnp.concatenate([chosen(got, k) for k in range(R)], axis=0)
        ma, la = a[:, DL : DL + 1], a[:, DL + 1 : DL + 2]
        mb, lb = stats_of(b, DL)
        m = jnp.maximum(ma, mb)
        wa, wb = jnp.exp2((ma - m) * EXPO), jnp.exp2((mb - m) * EXPO)
        o = a[:, :DL] * wa + b[:, :DL] * wb
        l = la * wa + lb * wb
        outs[n][:, :DL] = o.astype(outs[n].dtype)
        tile = stat_lanes(R * HB, (m, l) if n == 0 else split3(m) + split3(l))
        outs[n][:, DL:] = tile.astype(outs[n].dtype)


def combine_kernel(dims, *rest):
    CH, DL = dims
    outs = rest[CH:]
    *got, own = rest[:CH]
    x = [own[...]] + [v[...].astype(F32) for v in got]
    ms, ls = zip(*[(x[0][:, DL : DL + 1], x[0][:, DL + 1 : DL + 2])] + [stats_of(v, DL) for v in x[1:]])
    m = functools.reduce(jnp.maximum, ms)
    ws = [jnp.exp2((v - m) * EXPO) for v in ms]
    total = sum(w_ * l for w_, l in zip(ws, ls))
    o = (sum(w_ * v[:, :DL] for w_, v in zip(ws, x)) / total).astype(BF)
    at = 0
    for out in outs:
        out[...] = o[at : at + out.shape[0]]
        at += out.shape[0]


def value_kernel(dims, w, *rest):
    R, HC, HS, HB = dims
    n = R // 2 - 1
    far, *pairs, near, out = rest
    pairs = pairs[::-1]
    c = lax.axis_index("core")
    part = lax.rem(lax.axis_index("chip"), HS)
    ys = []
    for h in range(2):
        x = [v[...] for v in (near, far)] + [v[h * HB : (h + 1) * HB] for v in pairs]
        x = jnp.swapaxes(jnp.stack([v.astype(F32) for v in x]), 0, 1).astype(BF)
        first = h * HC + part * HB
        y = [jnp.dot(x[e], w[first + e], preferred_element_type=F32) for e in range(HB)]
        ys.append(jnp.swapaxes(jnp.stack(y), 0, 1).astype(BF))
        for i in range(n):
            out[2 + 2 * i + h] = ys[h][2 + i]
    for slot in range(2):
        out[slot] = jnp.where(c == 0, ys[0][slot], ys[1][slot])


def place_kernel(dims, assign, *rest):
    R, J, T, HC, HS, HB, CH = dims
    blocks, out = rest[: 2 * CH], rest[2 * CH]
    g, chip, c = lax.axis_index("req"), lax.axis_index("chip"), lax.axis_index("core")
    for n in range(CH):
        token = (chip ^ n) // HS
        j, t = token // T, lax.rem(token, T)
        for b in range(2):
            block = blocks[2 * (CH - 1 - n) + b]
            core, part = c ^ b, lax.rem(chip ^ n, HS)
            for slot in range(R):
                (k, h), (k1, h1) = units(R, 0)[slot], units(R, 1)[slot]
                k = k + core * (k1 - k)
                first = (h + core * (h1 - h)) * HC + part * HB
                request = assign[(g ^ k) * J + j]
                if HS == 1:
                    rows = pl.ds(pl.multiple_of(first, HB), HB)
                    out[t, request, rows, :] = block[slot]
                    continue
                for at in range(0, 2 * HC, HB):

                    @pl.when(first == at)
                    def _():
                        out[t, request, at : at + HB, :] = block[slot]


def body(
    q_nope, q_rope, w_uk, w_uv, latent_cache, rope_cache, positions,
    new_latent, new_rope, new_pos, lengths, assignment,
):
    T, REQS, HL, _ = q_nope.shape
    DL, DV = w_uk.shape[2], w_uv.shape[2]
    J, CAP = latent_cache.shape[:2]
    R, CH = lax.axis_size("req"), lax.axis_size("chip")
    HC = HL // 2
    HS = CH // (J * T)
    HB = HC // HS
    W = DL + LANES
    rates = turn_rates(DR)
    rate_row = jnp.asarray(np.tile(np.concatenate([rates, rates])[None], (R * J * T, 1)))
    rate_col = jnp.asarray(rates[:, None])
    assignment, new_pos, lengths = in_hbm(assignment), in_hbm(new_pos), in_hbm(lengths)
    big = pltpu.CompilerParams(vmem_limit_bytes=8 << 20)

    blocks = pl.pallas_call(
        functools.partial(absorb_kernel, (R, J, T, HC, DL)),
        out_shape=[jax.ShapeDtypeStruct((J, T, HC, W), BF)] * R,
        in_specs=[SMEM, SMEM, VMEM, HBM, HBM, HBM],
        out_specs=[VMEM] * R,
        scratch_shapes=[
            pltpu.VMEM((HC, DN, DL), BF),
            pltpu.VMEM(q_nope.shape, BF),
            pltpu.VMEM(q_rope.shape, BF),
            pltpu.SemaphoreType.DMA((6,)),
        ],
        compiler_params=big,
        name="absorb",
    )(assignment, new_pos, in_hbm(rate_row), in_hbm(q_nope), in_hbm(q_rope), in_hbm(w_uk))
    arrived = hops(blocks, "req")
    near = hop(blocks[0], "core", 1)

    cuts = CAP // 512
    keys, cached = pl.pallas_call(
        functools.partial(prepare_kernel, (J, T, CAP, DL), cuts),
        out_shape=[
            jax.ShapeDtypeStruct((J, KEYS, CAP + LANES), BF),
            jax.ShapeDtypeStruct((J, CAP + LANES, DL), BF),
        ],
        in_specs=[SMEM, SMEM, SMEM] + [VMEM] * 6 + [HBM],
        out_specs=[VMEM, VMEM],
        scratch_shapes=[pltpu.SemaphoreType.DMA((J, cuts))],
        compiler_params=pltpu.CompilerParams(vmem_limit_bytes=8 << 20),
        cost_estimate=pl.CostEstimate(
            flops=0, bytes_accessed=4 * J * CAP * DL, transcendentals=0
        ),
        name="prepare",
    )(
        assignment, lengths, new_pos, new_latent, new_rope, rate_row,
        positions, jnp.swapaxes(rope_cache, 1, 2), rate_col, in_hbm(latent_cache),
    )

    arrived, keys, cached = lax.optimization_barrier((arrived, keys, cached))
    own = arrived + [blocks[0]]
    other = [hop(v, "core", 1) for v in arrived] + [near]

    B = 1024
    NQ = T * R * HL
    send, keep = pl.pallas_call(
        functools.partial(attend_kernel, (R, J, T, HC, DL, CAP), B),
        out_shape=[
            jax.ShapeDtypeStruct((J, T, R, HC, W), BF),
            jax.ShapeDtypeStruct((J, T, R, HC, W), F32),
        ],
        in_specs=[VMEM] * (2 + 2 * R),
        out_specs=[VMEM, VMEM],
        scratch_shapes=[
            pltpu.VMEM((J, NQ, W), BF),
            pltpu.VMEM((2, NQ, B + LANES), F32),
            pltpu.VMEM((J, NQ, DL), F32),
        ],
        compiler_params=pltpu.CompilerParams(vmem_limit_bytes=16 << 20),
        name="attend",
    )(keys, cached, *own, *other)
    got = hop(send, "core", 1)
    pieces = pl.pallas_call(
        functools.partial(pair_kernel, (R, J, T, HC, HS, CH, DL)),
        out_shape=[jax.ShapeDtypeStruct((R * HB, W), BF if n else F32) for n in range(CH)],
        in_specs=[VMEM, VMEM],
        out_specs=[VMEM] * CH,
        compiler_params=big,
        name="pair",
    )(keep, got)
    shares = hops(pieces, "chip") + [pieces[0]]
    sizes = [HB, HB] + [2 * HB] * (R // 2 - 1)
    latents = pl.pallas_call(
        functools.partial(combine_kernel, (CH, DL)),
        out_shape=[jax.ShapeDtypeStruct((n, DL), BF) for n in sizes],
        in_specs=[VMEM] * CH,
        out_specs=[VMEM] * len(sizes),
        compiler_params=big,
        name="combine",
    )(*shares)
    far = hop(latents[1], "req", R - 1)
    crossed = [
        lax.ppermute(
            latents[1 + i],
            ("req", "core"),
            [(2 * g + c, 2 * (g ^ (2 * i - c)) + c) for g in range(R) for c in range(2)],
        )
        for i in reversed(range(1, R // 2))
    ]
    returned = [far] + crossed + [latents[0]]

    values = pl.pallas_call(
        functools.partial(value_kernel, (R, HC, HS, HB)),
        out_shape=jax.ShapeDtypeStruct((R, HB, DV), BF),
        in_specs=[VMEM] * (1 + len(returned)),
        out_specs=VMEM,
        compiler_params=big,
        name="value",
    )(w_uv, *returned)
    gathered = []
    for block in hops([values] * CH, "chip") + [values]:
        gathered += [block, hop(block, "core", 1)]
    return pl.pallas_call(
        functools.partial(place_kernel, (R, J, T, HC, HS, HB, CH)),
        out_shape=jax.ShapeDtypeStruct((T, REQS, HL, DV), BF),
        in_specs=[SMEM] + [VMEM] * (2 * CH),
        out_specs=VMEM,
        compiler_params=big,
        name="place",
    )(assignment, *gathered)


def solution(mesh):
    groups, shards = mesh.shape["req"], mesh.shape["seq"]
    cut = Mesh(mesh.devices.reshape(groups, shards // 2, 2), ("req", "chip", "core"))
    seq = ("chip", "core")
    in_specs = (
        P(None, None, "req", None),
        P(None, None, "req", None),
        P("req", None, None),
        P("req", None, None),
        P("req", seq, None),
        P("req", seq, None),
        P("req", seq),
        P(),
        P(),
        P(),
        P(),
        P(),
    )
    out_specs = P(None, None, "req", None)
    return jax.shard_map(body, mesh=cut, in_specs=in_specs, out_specs=out_specs, check_vma=False)
```

```python
import functools
import math

import jax
import jax.numpy as jnp
import numpy as np
from jax import lax
from jax.experimental import pallas as pl
from jax.experimental.pallas import tpu as pltpu
from jax.sharding import Mesh
from jax.sharding import PartitionSpec as P

DR = 64
DN = 128
LANES = 128
LOW = -1e30
EXPO = math.log2(math.e) / math.sqrt(DN + DR)
KEYS = 80
BF = jnp.bfloat16
F32 = jnp.float32
VMEM = pl.BlockSpec(memory_space=pltpu.VMEM)
SMEM = pl.BlockSpec(memory_space=pltpu.SMEM)
ANY = pl.BlockSpec(memory_space=pl.ANY)
HBM = pl.BlockSpec(memory_space=pltpu.HBM)


def in_hbm(x):
    return pltpu.with_memory_space_constraint(x, pltpu.HBM)


def hop(x, axis, n):
    size = lax.axis_size(axis)
    return lax.ppermute(x, axis, [(i, i ^ n) for i in range(size)])


def hops(blocks, axis):
    return [hop(blocks[k], axis, k) for k in reversed(range(1, len(blocks)))]


def turn_rates(width):
    half = width // 2
    slope = np.float32(-2.0 * math.log(10000.0) / width)
    frequency = np.exp(np.arange(half, dtype=np.float32) * slope).astype(np.float64)
    return np.round(frequency / (2.0 * math.pi) * 2.0**32).astype(np.int64).astype(np.int32)


def sin_cos(phase):
    x = phase.astype(F32) * np.float32(math.pi * 2.0**-32)
    z = x * x
    s = np.float32(2.7525562e-06)
    for c in (-0.00019840874, 0.0083333310, -0.16666667, 1.0):
        s = s * z + np.float32(c)
    s = s * x
    c = np.float32(-2.6051615e-07)
    for k in (2.4760495e-05, -0.0013888378, 0.041666638, -0.5, 1.0):
        c = c * z + np.float32(k)
    return 2.0 * s * c, 1.0 - 2.0 * s * s


def split3(x):
    a = x.astype(BF)
    r = x - a.astype(F32)
    b = r.astype(BF)
    return a.astype(F32), b.astype(F32), r - b.astype(F32)


def stat_lanes(rows, values):
    lane = lax.broadcasted_iota(jnp.int32, (rows, LANES), 1)
    tile = jnp.zeros((rows, LANES), F32)
    for i, v in enumerate(values):
        tile = jnp.where(lane == i, v, tile)
    return tile


def absorb_kernel(dims, assign, new_pos, rate, qn_hbm, qr_hbm, w_hbm, *rest):
    R, J, T, HC, DL = dims
    outs, wbuf, qn, qr, sem = rest[:R], *rest[R:]
    g, c = lax.axis_index("req"), lax.axis_index("core")
    piece = HC // 4
    inputs = [
        pltpu.make_async_copy(qn_hbm, qn, sem.at[4]),
        pltpu.make_async_copy(qr_hbm, qr, sem.at[5]),
    ]
    for copy in inputs:
        copy.start()
    copies = []
    for i in range(4):
        copies.append(
            pltpu.make_async_copy(
                w_hbm.at[pl.ds(c * HC + i * piece, piece)],
                wbuf.at[pl.ds(i * piece, piece)],
                sem.at[i],
            )
        )
        copies[-1].start()
    tokens = [(k, j, t) for k in range(R) for j in range(J) for t in range(T)]
    who = [assign[(g ^ k) * J + j] for k, j, t in tokens]
    half = pl.ds(pl.multiple_of(c * HC, HC), HC)
    row = lax.broadcasted_iota(jnp.int32, (len(tokens), DR), 0)
    pos = jnp.zeros((len(tokens), DR), jnp.int32)
    for i, (k, j, t) in enumerate(tokens):
        pos = jnp.where(row == i, new_pos[who[i]] + t, pos)
    sine, cosine = sin_cos(pos * rate[...])
    lane = lax.broadcasted_iota(jnp.int32, (len(tokens), DR), 1)
    sine = jnp.where(lane < DR // 2, -sine, sine)
    lane = lax.broadcasted_iota(jnp.int32, (HC, LANES - DR), 1)
    for copy in inputs:
        copy.wait()
    x = jnp.stack([qn[t, who[i], half, :].astype(F32) for i, (k, j, t) in enumerate(tokens)])
    x = jnp.swapaxes(x, 0, 1).astype(BF)
    for i, (k, j, t) in enumerate(tokens):
        v = qr[t, who[i], half, :].astype(F32)
        swapped = jnp.concatenate([v[:, DR // 2 :], v[:, : DR // 2]], axis=1)
        turned = v * cosine[i : i + 1] + swapped * sine[i : i + 1]
        one = ((lane == 0) | ((lane > t) & (lane < T))).astype(F32)
        outs[k][j, t, :, DL:] = jnp.concatenate([turned, one], axis=1).astype(BF)
    ys = []
    for h in range(HC):
        if h % piece == 0:
            copies[h // piece].wait()
        ys.append(jnp.dot(x[h], wbuf[h], preferred_element_type=F32))
    y = jnp.swapaxes(jnp.stack(ys), 0, 1).astype(BF)
    for i, (k, j, t) in enumerate(tokens):
        outs[k][j, t, :, :DL] = y[i]


def prepare_kernel(
    dims, cuts, assign, lengths, new_pos, new_lat, new_rope, rate_row,
    pos, rope, rate, c_hbm, out, c_out, sem,
):
    J, T, CAP, DL = dims
    g = lax.axis_index("req")
    shard = lax.axis_index("chip") * lax.axis_size("core") + lax.axis_index("core")
    half = DR // 2
    block = CAP // cuts
    copies = []
    for j in range(J):
        for i in range(cuts):
            rows = pl.ds(i * block, block)
            copies.append(
                pltpu.make_async_copy(c_hbm.at[j, rows], c_out.at[j, rows], sem.at[j, i])
            )
            copies[-1].start()
    sub = lax.broadcasted_iota(jnp.int32, (KEYS - DR, block), 0)
    turn = rate[...]
    for j in range(J):
        end = lengths[assign[g * J + j]] - shard * CAP

        def rotate(i, carry):
            at = pl.ds(pl.multiple_of(i * block, LANES), block)
            sine, cosine = sin_cos(pos[j : j + 1, at] * turn)
            a = rope[j, :half, at].astype(F32)
            b = rope[j, half:, at].astype(F32)
            out[j, :half, at] = (a * cosine - b * sine).astype(BF)
            out[j, half:DR, at] = (b * cosine + a * sine).astype(BF)
            bad = i * block + lax.broadcasted_iota(jnp.int32, (1, block), 1) >= end
            out[j, DR:, at] = jnp.where((sub == 0) & bad, LOW, 0.0).astype(BF)
            return carry

        lax.fori_loop(0, cuts, rotate, 0)
    for j in range(J):
        r = assign[g * J + j]
        pick = lax.broadcasted_iota(jnp.int32, new_lat.shape[1:], 0) == r
        lat = [
            jnp.sum(jnp.where(pick, new_lat[u].astype(F32), 0.0), axis=0, keepdims=True)
            for u in range(T)
        ]
        pick = lax.broadcasted_iota(jnp.int32, new_rope.shape[1:], 0) == r
        rop = [
            jnp.sum(jnp.where(pick, new_rope[u].astype(F32), 0.0), axis=0, keepdims=True)
            for u in range(T)
        ]
        lat = jnp.concatenate(lat + [jnp.zeros((LANES - T, DL), F32)], axis=0)
        c_out[j, CAP:, :] = lat.astype(BF)
        rop = jnp.concatenate(rop + [jnp.zeros((8 - T, DR), F32)], axis=0)
        step = lax.broadcasted_iota(jnp.int32, (8, DR), 0)
        lane = lax.broadcasted_iota(jnp.int32, (8, DR), 1)
        sine, cosine = sin_cos((new_pos[r] + step) * rate_row[:8])
        sine = jnp.where(lane < DR // 2, -sine, sine)
        swapped = jnp.concatenate([rop[:, DR // 2 :], rop[:, : DR // 2]], axis=1)
        rop = rop * cosine + swapped * sine
        rop = jnp.concatenate([rop, jnp.zeros((LANES - 8, DR), F32)], axis=0)
        u = lax.broadcasted_iota(jnp.int32, (LANES, LANES - DR), 0)
        lane = lax.broadcasted_iota(jnp.int32, (LANES, LANES - DR), 1)
        absent = (lane == 0) & ((u >= T) | (shard > 0))
        later = (lane > 0) & (lane == u) & (u < T)
        rop = jnp.concatenate([rop, jnp.where(absent | later, LOW, 0.0)], axis=1)
        out[j, :, CAP:] = jnp.transpose(rop)[:KEYS].astype(BF)
    for copy in copies:
        copy.wait()


def units(R, c):
    found = [(0, c), (1, c)]
    for i in range(1, R // 2):
        found += [(2 * i + c, 0), (2 * i + c, 1)]
    return found


def attend_kernel(dims, B, keys, cbuf, *rest):
    R, J, T, HC, DL, CAP = dims
    own, other = rest[:R][::-1], rest[R : 2 * R][::-1]
    send, keep, q, sbuf, acc = rest[2 * R :]
    nb = CAP // B
    NQ = T * R * 2 * HC
    c = lax.axis_index("core")
    for j in range(J):
        for t in range(T):
            for k in range(R):
                mine, theirs = own[k][j, t], other[k][j, t]
                base = (t * R + k) * 2 * HC
                q[j, base : base + HC, :] = jnp.where(c == 0, mine, theirs)
                q[j, base + HC : base + 2 * HC, :] = jnp.where(c == 0, theirs, mine)
    nt = (((1,), (1,)), ((), ()))
    blocks = [
        (j, pl.ds(i * B, B + (LANES if i == nb - 1 else 0))) for j in range(J) for i in range(nb)
    ]

    def score(n):
        j, rows = blocks[n]
        s = lax.dot_general(q[j, :, :DL], cbuf[j, rows], nt, preferred_element_type=F32)
        s = s + jnp.dot(
            q[j, :, DL : DL + KEYS], keys[j, :, rows], preferred_element_type=F32
        )
        sbuf[n % 2, :, : rows.size] = s

    score(0)
    for n, (j, rows) in enumerate(blocks):
        if n + 1 < len(blocks):
            score(n + 1)
        s = sbuf[n % 2, :, : rows.size]
        top = jnp.max(s, axis=1, keepdims=True)
        if n % nb:
            top = jnp.maximum(m, top)
        p = jnp.exp2(s * EXPO - top * EXPO)
        part = jnp.sum(p, axis=1, keepdims=True)
        value = jnp.dot(p.astype(BF), cbuf[j, rows], preferred_element_type=F32)
        if n % nb:
            shrink = jnp.exp2((m - top) * EXPO)
            l = l * shrink + part
            acc[j] = acc[j] * shrink + value
        else:
            l = part
            acc[j] = value
        m = top
        if n % nb < nb - 1:
            continue
        whole = stat_lanes(NQ, (m, l))
        parts = stat_lanes(NQ, split3(m) + split3(l))
        for t in range(T):
            for slot in range(R):
                lo, hi = [
                    slice((t * R + k) * 2 * HC + h * HC, (t * R + k) * 2 * HC + (h + 1) * HC)
                    for k, h in (units(R, 0)[slot], units(R, 1)[slot])
                ]
                keep[j, t, slot, :, :DL] = jnp.where(c == 0, acc[j, lo], acc[j, hi])
                send[j, t, slot, :, :DL] = jnp.where(c == 0, acc[j, hi], acc[j, lo]).astype(BF)
                keep[j, t, slot, :, DL:] = jnp.where(c == 0, whole[lo], whole[hi])
                send[j, t, slot, :, DL:] = jnp.where(c == 0, parts[hi], parts[lo]).astype(BF)


def stats_of(x, DL):
    m = x[:, DL : DL + 1] + x[:, DL + 1 : DL + 2] + x[:, DL + 2 : DL + 3]
    return m, x[:, DL + 3 : DL + 4] + x[:, DL + 4 : DL + 5] + x[:, DL + 5 : DL + 6]


def pair_kernel(dims, keep, got, *outs):
    R, J, T, HC, HS, CH, DL = dims
    HB = HC // HS
    chip = lax.axis_index("chip")
    for n in range(CH):
        token = (chip ^ n) // HS
        j, t = token // T, lax.rem(token, T)
        part = lax.rem(chip ^ n, HS)

        def chosen(ref, k):
            v = ref[j, t, k].astype(F32)
            rows = v[:HB]
            for s in range(1, HS):
                rows = jnp.where(part == s, v[s * HB : (s + 1) * HB], rows)
            return rows

        a = jnp.concatenate([chosen(keep, k) for k in range(R)], axis=0)
        b = jnp.concatenate([chosen(got, k) for k in range(R)], axis=0)
        ma, la = a[:, DL : DL + 1], a[:, DL + 1 : DL + 2]
        mb, lb = stats_of(b, DL)
        m = jnp.maximum(ma, mb)
        wa, wb = jnp.exp2((ma - m) * EXPO), jnp.exp2((mb - m) * EXPO)
        o = a[:, :DL] * wa + b[:, :DL] * wb
        l = la * wa + lb * wb
        outs[n][:, :DL] = o.astype(outs[n].dtype)
        tile = stat_lanes(R * HB, (m, l) if n == 0 else split3(m) + split3(l))
        outs[n][:, DL:] = tile.astype(outs[n].dtype)


def combine_kernel(dims, *rest):
    CH, DL = dims
    outs = rest[CH:]
    *got, own = rest[:CH]
    x = [own[...]] + [v[...].astype(F32) for v in got]
    ms, ls = zip(*[(x[0][:, DL : DL + 1], x[0][:, DL + 1 : DL + 2])] + [stats_of(v, DL) for v in x[1:]])
    m = functools.reduce(jnp.maximum, ms)
    ws = [jnp.exp2((v - m) * EXPO) for v in ms]
    total = sum(w_ * l for w_, l in zip(ws, ls))
    o = (sum(w_ * v[:, :DL] for w_, v in zip(ws, x)) / total).astype(BF)
    at = 0
    for out in outs:
        out[...] = o[at : at + out.shape[0]]
        at += out.shape[0]


def value_kernel(dims, w, *rest):
    R, HC, HS, HB = dims
    n = R // 2 - 1
    *pairs, beside, near, out = rest
    pairs = pairs[::-1]
    c = lax.axis_index("core")
    part = lax.rem(lax.axis_index("chip"), HS)
    ys = []
    for h in range(2):
        x = [v[...] for v in (near, beside)] + [v[h * HB : (h + 1) * HB] for v in pairs]
        x = jnp.swapaxes(jnp.stack([v.astype(F32) for v in x]), 0, 1).astype(BF)
        first = h * HC + part * HB
        y = [jnp.dot(x[e], w[first + e], preferred_element_type=F32) for e in range(HB)]
        ys.append(jnp.swapaxes(jnp.stack(y), 0, 1).astype(BF))
        for i in range(n):
            out[2 + 2 * i + h] = ys[h][2 + i]
    for slot in range(2):
        out[slot] = jnp.where(c == 0, ys[0][slot], ys[1][slot])


def place_kernel(dims, assign, *rest):
    R, J, T, HC, HS, HB, CH = dims
    *blocks, beside, mine, out = rest
    g, chip, c = lax.axis_index("req"), lax.axis_index("chip"), lax.axis_index("core")
    for n in range(CH):
        token = (chip ^ n) // HS
        j, t = token // T, lax.rem(token, T)
        for b in range(2):
            block = (mine, beside)[n].at[b] if n < 2 else blocks[2 * (n - 2) + b]
            core, part = c ^ b, lax.rem(chip ^ n, HS)
            for slot in range(R):
                (k, h), (k1, h1) = units(R, 0)[slot], units(R, 1)[slot]
                k = k + core * (k1 - k)
                first = (h + core * (h1 - h)) * HC + part * HB
                request = assign[(g ^ k) * J + j]
                if HS == 1:
                    rows = pl.ds(pl.multiple_of(first, HB), HB)
                    out[t, request, rows, :] = block[slot]
                    continue
                for at in range(0, 2 * HC, HB):

                    @pl.when(first == at)
                    def _():
                        out[t, request, at : at + HB, :] = block[slot]


def body(
    q_nope, q_rope, w_uk, w_uv, latent_cache, rope_cache, positions,
    new_latent, new_rope, new_pos, lengths, assignment,
):
    T, REQS, HL, _ = q_nope.shape
    DL, DV = w_uk.shape[2], w_uv.shape[2]
    J, CAP = latent_cache.shape[:2]
    R, CH = lax.axis_size("req"), lax.axis_size("chip")
    HC = HL // 2
    HS = CH // (J * T)
    HB = HC // HS
    W = DL + LANES
    rates = turn_rates(DR)
    rate_row = jnp.asarray(np.tile(np.concatenate([rates, rates])[None], (R * J * T, 1)))
    rate_col = jnp.asarray(rates[:, None])
    assignment, new_pos, lengths = in_hbm(assignment), in_hbm(new_pos), in_hbm(lengths)
    big = pltpu.CompilerParams(vmem_limit_bytes=8 << 20)

    blocks = pl.pallas_call(
        functools.partial(absorb_kernel, (R, J, T, HC, DL)),
        out_shape=[jax.ShapeDtypeStruct((J, T, HC, W), BF)] * R,
        in_specs=[SMEM, SMEM, VMEM, HBM, HBM, HBM],
        out_specs=[VMEM] * R,
        scratch_shapes=[
            pltpu.VMEM((HC, DN, DL), BF),
            pltpu.VMEM(q_nope.shape, BF),
            pltpu.VMEM(q_rope.shape, BF),
            pltpu.SemaphoreType.DMA((6,)),
        ],
        compiler_params=big,
        name="absorb",
    )(assignment, new_pos, in_hbm(rate_row), in_hbm(q_nope), in_hbm(q_rope), in_hbm(w_uk))
    arrived = hops(blocks, "req")
    near = hop(blocks[0], "core", 1)

    cuts = CAP // 512
    keys, cached = pl.pallas_call(
        functools.partial(prepare_kernel, (J, T, CAP, DL), cuts),
        out_shape=[
            jax.ShapeDtypeStruct((J, KEYS, CAP + LANES), BF),
            jax.ShapeDtypeStruct((J, CAP + LANES, DL), BF),
        ],
        in_specs=[SMEM, SMEM, SMEM] + [VMEM] * 6 + [HBM],
        out_specs=[VMEM, VMEM],
        scratch_shapes=[pltpu.SemaphoreType.DMA((J, cuts))],
        compiler_params=pltpu.CompilerParams(vmem_limit_bytes=8 << 20),
        cost_estimate=pl.CostEstimate(
            flops=0, bytes_accessed=4 * J * CAP * DL, transcendentals=0
        ),
        name="prepare",
    )(
        assignment, lengths, new_pos, new_latent, new_rope, rate_row,
        positions, jnp.swapaxes(rope_cache, 1, 2), rate_col, in_hbm(latent_cache),
    )

    arrived, keys, cached = lax.optimization_barrier((arrived, keys, cached))
    own = arrived + [blocks[0]]
    other = [hop(v, "core", 1) for v in arrived] + [near]

    B = 1024
    NQ = T * R * HL
    send, keep = pl.pallas_call(
        functools.partial(attend_kernel, (R, J, T, HC, DL, CAP), B),
        out_shape=[
            jax.ShapeDtypeStruct((J, T, R, HC, W), BF),
            jax.ShapeDtypeStruct((J, T, R, HC, W), F32),
        ],
        in_specs=[VMEM] * (2 + 2 * R),
        out_specs=[VMEM, VMEM],
        scratch_shapes=[
            pltpu.VMEM((J, NQ, W), BF),
            pltpu.VMEM((2, NQ, B + LANES), F32),
            pltpu.VMEM((J, NQ, DL), F32),
        ],
        compiler_params=pltpu.CompilerParams(vmem_limit_bytes=16 << 20),
        name="attend",
    )(keys, cached, *own, *other)
    got = hop(send, "core", 1)
    pieces = pl.pallas_call(
        functools.partial(pair_kernel, (R, J, T, HC, HS, CH, DL)),
        out_shape=[jax.ShapeDtypeStruct((R * HB, W), BF if n else F32) for n in range(CH)],
        in_specs=[VMEM, VMEM],
        out_specs=[VMEM] * CH,
        compiler_params=big,
        name="pair",
    )(keep, got)
    shares = hops(pieces, "chip") + [pieces[0]]
    sizes = [HB, HB] + [2 * HB] * (R // 2 - 1)
    latents = pl.pallas_call(
        functools.partial(combine_kernel, (CH, DL)),
        out_shape=[jax.ShapeDtypeStruct((n, DL), BF) for n in sizes],
        in_specs=[VMEM] * CH,
        out_specs=[VMEM] * len(sizes),
        compiler_params=big,
        name="combine",
    )(*shares)
    returned = [
        lax.ppermute(
            latents[1 + i],
            ("req", "core"),
            [(2 * g + c, 2 * (g ^ (2 * i + c)) + c) for g in range(R) for c in range(2)],
        )
        for i in reversed(range(1, R // 2))
    ]
    returned += [hop(latents[1], "req", 1), latents[0]]

    values = pl.pallas_call(
        functools.partial(value_kernel, (R, HC, HS, HB)),
        out_shape=jax.ShapeDtypeStruct((R, HB, DV), BF),
        in_specs=[VMEM] * (1 + len(returned)),
        out_specs=VMEM,
        compiler_params=big,
        name="value",
    )(w_uv, *returned)
    gathered = []
    for n in range(2, CH):
        block = hop(values, "chip", n)
        gathered += [block, hop(block, "core", 1)]
    both = jnp.stack([values, hop(values, "core", 1)])
    gathered += [hop(both, "chip", 1), both]
    return pl.pallas_call(
        functools.partial(place_kernel, (R, J, T, HC, HS, HB, CH)),
        out_shape=jax.ShapeDtypeStruct((T, REQS, HL, DV), BF),
        in_specs=[SMEM] + [VMEM] * len(gathered),
        out_specs=VMEM,
        compiler_params=big,
        name="place",
    )(assignment, *gathered)


def solution(mesh):
    groups, shards = mesh.shape["req"], mesh.shape["seq"]
    cut = Mesh(mesh.devices.reshape(groups, shards // 2, 2), ("req", "chip", "core"))
    seq = ("chip", "core")
    in_specs = (
        P(None, None, "req", None),
        P(None, None, "req", None),
        P("req", None, None),
        P("req", None, None),
        P("req", seq, None),
        P("req", seq, None),
        P("req", seq),
        P(),
        P(),
        P(),
        P(),
        P(),
    )
    out_specs = P(None, None, "req", None)
    return jax.shard_map(body, mesh=cut, in_specs=in_specs, out_specs=out_specs, check_vma=False)
```

```python
import functools
import math

import jax
import jax.numpy as jnp
import numpy as np
from jax import lax
from jax.experimental import pallas as pl
from jax.experimental.pallas import tpu as pltpu
from jax.sharding import Mesh
from jax.sharding import PartitionSpec as P

DR = 64
DN = 128
LANES = 128
LOW = -1e30
EXPO = math.log2(math.e) / math.sqrt(DN + DR)
KEYS = 80
BF = jnp.bfloat16
F32 = jnp.float32
VMEM = pl.BlockSpec(memory_space=pltpu.VMEM)
SMEM = pl.BlockSpec(memory_space=pltpu.SMEM)
ANY = pl.BlockSpec(memory_space=pl.ANY)
HBM = pl.BlockSpec(memory_space=pltpu.HBM)


def in_hbm(x):
    return pltpu.with_memory_space_constraint(x, pltpu.HBM)


def hop(x, axis, n):
    size = lax.axis_size(axis)
    return lax.ppermute(x, axis, [(i, i ^ n) for i in range(size)])


def hops(blocks, axis):
    return [hop(blocks[k], axis, k) for k in reversed(range(1, len(blocks)))]


def turn_rates(width):
    half = width // 2
    slope = np.float32(-2.0 * math.log(10000.0) / width)
    frequency = np.exp(np.arange(half, dtype=np.float32) * slope).astype(np.float64)
    return np.round(frequency / (2.0 * math.pi) * 2.0**32).astype(np.int64).astype(np.int32)


def sin_cos(phase):
    x = phase.astype(F32) * np.float32(math.pi * 2.0**-32)
    z = x * x
    s = np.float32(2.7525562e-06)
    for c in (-0.00019840874, 0.0083333310, -0.16666667, 1.0):
        s = s * z + np.float32(c)
    s = s * x
    c = np.float32(-2.6051615e-07)
    for k in (2.4760495e-05, -0.0013888378, 0.041666638, -0.5, 1.0):
        c = c * z + np.float32(k)
    return 2.0 * s * c, 1.0 - 2.0 * s * s


def split3(x):
    a = x.astype(BF)
    r = x - a.astype(F32)
    b = r.astype(BF)
    return a.astype(F32), b.astype(F32), r - b.astype(F32)


def stat_lanes(rows, values):
    lane = lax.broadcasted_iota(jnp.int32, (rows, LANES), 1)
    tile = jnp.zeros((rows, LANES), F32)
    for i, v in enumerate(values):
        tile = jnp.where(lane == i, v, tile)
    return tile


def absorb_kernel(dims, assign, new_pos, rate, qn_hbm, qr_hbm, w_hbm, *rest):
    R, J, T, HC, DL = dims
    outs, wbuf, qn, qr, sem = rest[:R], *rest[R:]
    g, c = lax.axis_index("req"), lax.axis_index("core")
    piece = HC // 4
    inputs = [
        pltpu.make_async_copy(qn_hbm, qn, sem.at[4]),
        pltpu.make_async_copy(qr_hbm, qr, sem.at[5]),
    ]
    for copy in inputs:
        copy.start()
    copies = []
    for i in range(4):
        copies.append(
            pltpu.make_async_copy(
                w_hbm.at[pl.ds(c * HC + i * piece, piece)],
                wbuf.at[pl.ds(i * piece, piece)],
                sem.at[i],
            )
        )
        copies[-1].start()
    tokens = [(k, j, t) for k in range(R) for j in range(J) for t in range(T)]
    who = [assign[(g ^ k) * J + j] for k, j, t in tokens]
    half = pl.ds(pl.multiple_of(c * HC, HC), HC)
    row = lax.broadcasted_iota(jnp.int32, (len(tokens), DR), 0)
    pos = jnp.zeros((len(tokens), DR), jnp.int32)
    for i, (k, j, t) in enumerate(tokens):
        pos = jnp.where(row == i, new_pos[who[i]] + t, pos)
    sine, cosine = sin_cos(pos * rate[...])
    lane = lax.broadcasted_iota(jnp.int32, (len(tokens), DR), 1)
    sine = jnp.where(lane < DR // 2, -sine, sine)
    lane = lax.broadcasted_iota(jnp.int32, (HC, LANES - DR), 1)
    for copy in inputs:
        copy.wait()
    x = jnp.stack([qn[t, who[i], half, :].astype(F32) for i, (k, j, t) in enumerate(tokens)])
    x = jnp.swapaxes(x, 0, 1).astype(BF)
    for i, (k, j, t) in enumerate(tokens):
        v = qr[t, who[i], half, :].astype(F32)
        swapped = jnp.concatenate([v[:, DR // 2 :], v[:, : DR // 2]], axis=1)
        turned = v * cosine[i : i + 1] + swapped * sine[i : i + 1]
        one = ((lane == 0) | ((lane > t) & (lane < T))).astype(F32)
        outs[k][j, t, :, DL:] = jnp.concatenate([turned, one], axis=1).astype(BF)
    ys = []
    for h in range(HC):
        if h % piece == 0:
            copies[h // piece].wait()
        ys.append(jnp.dot(x[h], wbuf[h], preferred_element_type=F32))
    y = jnp.swapaxes(jnp.stack(ys), 0, 1).astype(BF)
    for i, (k, j, t) in enumerate(tokens):
        outs[k][j, t, :, :DL] = y[i]


def prepare_kernel(
    dims, cuts, assign, lengths, new_pos, new_lat, new_rope, rate_row,
    pos, rope, rate, c_hbm, out, c_out, sem,
):
    J, T, CAP, DL = dims
    g = lax.axis_index("req")
    shard = lax.axis_index("chip") * lax.axis_size("core") + lax.axis_index("core")
    half = DR // 2
    block = CAP // cuts
    copies = []
    for j in range(J):
        for i in range(cuts):
            rows = pl.ds(i * block, block)
            copies.append(
                pltpu.make_async_copy(c_hbm.at[j, rows], c_out.at[j, rows], sem.at[j, i])
            )
            copies[-1].start()
    sub = lax.broadcasted_iota(jnp.int32, (KEYS - DR, block), 0)
    turn = rate[...]
    for j in range(J):
        end = lengths[assign[g * J + j]] - shard * CAP

        def rotate(i, carry):
            at = pl.ds(pl.multiple_of(i * block, LANES), block)
            sine, cosine = sin_cos(pos[j : j + 1, at] * turn)
            a = rope[j, :half, at].astype(F32)
            b = rope[j, half:, at].astype(F32)
            out[j, :half, at] = (a * cosine - b * sine).astype(BF)
            out[j, half:DR, at] = (b * cosine + a * sine).astype(BF)
            bad = i * block + lax.broadcasted_iota(jnp.int32, (1, block), 1) >= end
            out[j, DR:, at] = jnp.where((sub == 0) & bad, LOW, 0.0).astype(BF)
            return carry

        lax.fori_loop(0, cuts, rotate, 0)
    for j in range(J):
        r = assign[g * J + j]
        pick = lax.broadcasted_iota(jnp.int32, new_lat.shape[1:], 0) == r
        lat = [
            jnp.sum(jnp.where(pick, new_lat[u].astype(F32), 0.0), axis=0, keepdims=True)
            for u in range(T)
        ]
        pick = lax.broadcasted_iota(jnp.int32, new_rope.shape[1:], 0) == r
        rop = [
            jnp.sum(jnp.where(pick, new_rope[u].astype(F32), 0.0), axis=0, keepdims=True)
            for u in range(T)
        ]
        lat = jnp.concatenate(lat + [jnp.zeros((LANES - T, DL), F32)], axis=0)
        c_out[j, CAP:, :] = lat.astype(BF)
        rop = jnp.concatenate(rop + [jnp.zeros((8 - T, DR), F32)], axis=0)
        step = lax.broadcasted_iota(jnp.int32, (8, DR), 0)
        lane = lax.broadcasted_iota(jnp.int32, (8, DR), 1)
        sine, cosine = sin_cos((new_pos[r] + step) * rate_row[:8])
        sine = jnp.where(lane < DR // 2, -sine, sine)
        swapped = jnp.concatenate([rop[:, DR // 2 :], rop[:, : DR // 2]], axis=1)
        rop = rop * cosine + swapped * sine
        rop = jnp.concatenate([rop, jnp.zeros((LANES - 8, DR), F32)], axis=0)
        u = lax.broadcasted_iota(jnp.int32, (LANES, LANES - DR), 0)
        lane = lax.broadcasted_iota(jnp.int32, (LANES, LANES - DR), 1)
        absent = (lane == 0) & ((u >= T) | (shard > 0))
        later = (lane > 0) & (lane == u) & (u < T)
        rop = jnp.concatenate([rop, jnp.where(absent | later, LOW, 0.0)], axis=1)
        out[j, :, CAP:] = jnp.transpose(rop)[:KEYS].astype(BF)
    for copy in copies:
        copy.wait()


def units(R, c):
    found = [(0, c), (1, c)]
    for i in range(1, R // 2):
        found += [(2 * i + c, 0), (2 * i + c, 1)]
    return found


def attend_kernel(dims, B, keys, cbuf, *rest):
    R, J, T, HC, DL, CAP = dims
    own, other = rest[:R][::-1], rest[R : 2 * R][::-1]
    send, keep, q, sbuf, acc = rest[2 * R :]
    NQ = T * R * 2 * HC
    c = lax.axis_index("core")
    for j in range(J):
        for t in range(T):
            for k in range(R):
                mine, theirs = own[k][j, t], other[k][j, t]
                base = (t * R + k) * 2 * HC
                q[j, base : base + HC, :] = jnp.where(c == 0, mine, theirs)
                q[j, base + HC : base + 2 * HC, :] = jnp.where(c == 0, theirs, mine)
    nt = (((1,), (1,)), ((), ()))
    cuts = [0, *range(B // 2, CAP, B), CAP + LANES]
    nb = len(cuts) - 1
    blocks = [
        (j, pl.ds(cuts[i], cuts[i + 1] - cuts[i])) for j in range(J) for i in range(nb)
    ]

    def score(n):
        j, rows = blocks[n]
        s = lax.dot_general(q[j, :, :DL], cbuf[j, rows], nt, preferred_element_type=F32)
        s = s + jnp.dot(
            q[j, :, DL : DL + KEYS], keys[j, :, rows], preferred_element_type=F32
        )
        sbuf[n % 2, :, : rows.size] = s

    score(0)
    for n, (j, rows) in enumerate(blocks):
        if n + 1 < len(blocks):
            score(n + 1)
        s = sbuf[n % 2, :, : rows.size]
        top = jnp.max(s, axis=1, keepdims=True)
        if n % nb:
            top = jnp.maximum(m, top)
        p = jnp.exp2(s * EXPO - top * EXPO)
        part = jnp.sum(p, axis=1, keepdims=True)
        value = jnp.dot(p.astype(BF), cbuf[j, rows], preferred_element_type=F32)
        if n % nb:
            shrink = jnp.exp2((m - top) * EXPO)
            l = l * shrink + part
            acc[j] = acc[j] * shrink + value
        else:
            l = part
            acc[j] = value
        m = top
        if n % nb < nb - 1:
            continue
        whole = stat_lanes(NQ, (m, l))
        parts = stat_lanes(NQ, split3(m) + split3(l))
        for t in range(T):
            for slot in range(R):
                lo, hi = [
                    slice((t * R + k) * 2 * HC + h * HC, (t * R + k) * 2 * HC + (h + 1) * HC)
                    for k, h in (units(R, 0)[slot], units(R, 1)[slot])
                ]
                keep[j, t, slot, :, :DL] = jnp.where(c == 0, acc[j, lo], acc[j, hi])
                send[j, t, slot, :, :DL] = jnp.where(c == 0, acc[j, hi], acc[j, lo]).astype(BF)
                keep[j, t, slot, :, DL:] = jnp.where(c == 0, whole[lo], whole[hi])
                send[j, t, slot, :, DL:] = jnp.where(c == 0, parts[hi], parts[lo]).astype(BF)


def stats_of(x, DL):
    m = x[:, DL : DL + 1] + x[:, DL + 1 : DL + 2] + x[:, DL + 2 : DL + 3]
    return m, x[:, DL + 3 : DL + 4] + x[:, DL + 4 : DL + 5] + x[:, DL + 5 : DL + 6]


def pair_kernel(dims, keep, got, *outs):
    R, J, T, HC, HS, CH, DL = dims
    HB = HC // HS
    chip = lax.axis_index("chip")
    for n in range(CH):
        token = (chip ^ n) // HS
        j, t = token // T, lax.rem(token, T)
        part = lax.rem(chip ^ n, HS)

        def chosen(ref, k):
            v = ref[j, t, k].astype(F32)
            rows = v[:HB]
            for s in range(1, HS):
                rows = jnp.where(part == s, v[s * HB : (s + 1) * HB], rows)
            return rows

        a = jnp.concatenate([chosen(keep, k) for k in range(R)], axis=0)
        b = jnp.concatenate([chosen(got, k) for k in range(R)], axis=0)
        ma, la = a[:, DL : DL + 1], a[:, DL + 1 : DL + 2]
        mb, lb = stats_of(b, DL)
        m = jnp.maximum(ma, mb)
        wa, wb = jnp.exp2((ma - m) * EXPO), jnp.exp2((mb - m) * EXPO)
        o = a[:, :DL] * wa + b[:, :DL] * wb
        l = la * wa + lb * wb
        outs[n][:, :DL] = o.astype(outs[n].dtype)
        tile = stat_lanes(R * HB, (m, l) if n == 0 else split3(m) + split3(l))
        outs[n][:, DL:] = tile.astype(outs[n].dtype)


def combine_kernel(dims, *rest):
    CH, DL = dims
    outs = rest[CH:]
    *got, own = rest[:CH]
    x = [own[...]] + [v[...].astype(F32) for v in got]
    ms, ls = zip(*[(x[0][:, DL : DL + 1], x[0][:, DL + 1 : DL + 2])] + [stats_of(v, DL) for v in x[1:]])
    m = functools.reduce(jnp.maximum, ms)
    ws = [jnp.exp2((v - m) * EXPO) for v in ms]
    total = sum(w_ * l for w_, l in zip(ws, ls))
    o = (sum(w_ * v[:, :DL] for w_, v in zip(ws, x)) / total).astype(BF)
    at = 0
    for out in outs:
        out[...] = o[at : at + out.shape[0]]
        at += out.shape[0]


def value_kernel(dims, w, *rest):
    R, HC, HS, HB = dims
    n = R // 2 - 1
    *pairs, beside, near, out = rest
    pairs = pairs[::-1]
    c = lax.axis_index("core")
    part = lax.rem(lax.axis_index("chip"), HS)
    ys = []
    for h in range(2):
        x = [v[...] for v in (near, beside)] + [v[h * HB : (h + 1) * HB] for v in pairs]
        x = jnp.swapaxes(jnp.stack([v.astype(F32) for v in x]), 0, 1).astype(BF)
        first = h * HC + part * HB
        y = [jnp.dot(x[e], w[first + e], preferred_element_type=F32) for e in range(HB)]
        ys.append(jnp.swapaxes(jnp.stack(y), 0, 1).astype(BF))
        for i in range(n):
            out[2 + 2 * i + h] = ys[h][2 + i]
    for slot in range(2):
        out[slot] = jnp.where(c == 0, ys[0][slot], ys[1][slot])


def place_kernel(dims, assign, *rest):
    R, J, T, HC, HS, HB, CH = dims
    *blocks, beside, mine, out = rest
    g, chip, c = lax.axis_index("req"), lax.axis_index("chip"), lax.axis_index("core")
    for n in range(CH):
        token = (chip ^ n) // HS
        j, t = token // T, lax.rem(token, T)
        for b in range(2):
            block = (mine, beside)[n].at[b] if n < 2 else blocks[2 * (n - 2) + b]
            core, part = c ^ b, lax.rem(chip ^ n, HS)
            for slot in range(R):
                (k, h), (k1, h1) = units(R, 0)[slot], units(R, 1)[slot]
                k = k + core * (k1 - k)
                first = (h + core * (h1 - h)) * HC + part * HB
                request = assign[(g ^ k) * J + j]
                if HS == 1:
                    rows = pl.ds(pl.multiple_of(first, HB), HB)
                    out[t, request, rows, :] = block[slot]
                    continue
                for at in range(0, 2 * HC, HB):

                    @pl.when(first == at)
                    def _():
                        out[t, request, at : at + HB, :] = block[slot]


def body(
    q_nope, q_rope, w_uk, w_uv, latent_cache, rope_cache, positions,
    new_latent, new_rope, new_pos, lengths, assignment,
):
    T, REQS, HL, _ = q_nope.shape
    DL, DV = w_uk.shape[2], w_uv.shape[2]
    J, CAP = latent_cache.shape[:2]
    R, CH = lax.axis_size("req"), lax.axis_size("chip")
    HC = HL // 2
    HS = CH // (J * T)
    HB = HC // HS
    W = DL + LANES
    rates = turn_rates(DR)
    rate_row = jnp.asarray(np.tile(np.concatenate([rates, rates])[None], (R * J * T, 1)))
    rate_col = jnp.asarray(rates[:, None])
    places = assignment
    assignment, new_pos, lengths = in_hbm(assignment), in_hbm(new_pos), in_hbm(lengths)
    big = pltpu.CompilerParams(vmem_limit_bytes=8 << 20)

    blocks = pl.pallas_call(
        functools.partial(absorb_kernel, (R, J, T, HC, DL)),
        out_shape=[jax.ShapeDtypeStruct((J, T, HC, W), BF)] * R,
        in_specs=[SMEM, SMEM, VMEM, HBM, HBM, HBM],
        out_specs=[VMEM] * R,
        scratch_shapes=[
            pltpu.VMEM((HC, DN, DL), BF),
            pltpu.VMEM(q_nope.shape, BF),
            pltpu.VMEM(q_rope.shape, BF),
            pltpu.SemaphoreType.DMA((6,)),
        ],
        compiler_params=big,
        name="absorb",
    )(assignment, new_pos, in_hbm(rate_row), in_hbm(q_nope), in_hbm(q_rope), in_hbm(w_uk))
    arrived = hops(blocks, "req")
    near = hop(blocks[0], "core", 1)

    cuts = CAP // 512
    keys, cached = pl.pallas_call(
        functools.partial(prepare_kernel, (J, T, CAP, DL), cuts),
        out_shape=[
            jax.ShapeDtypeStruct((J, KEYS, CAP + LANES), BF),
            jax.ShapeDtypeStruct((J, CAP + LANES, DL), BF),
        ],
        in_specs=[SMEM, SMEM, SMEM] + [VMEM] * 6 + [HBM],
        out_specs=[VMEM, VMEM],
        scratch_shapes=[pltpu.SemaphoreType.DMA((J, cuts))],
        compiler_params=pltpu.CompilerParams(vmem_limit_bytes=8 << 20),
        cost_estimate=pl.CostEstimate(
            flops=0, bytes_accessed=4 * J * CAP * DL, transcendentals=0
        ),
        name="prepare",
    )(
        assignment, lengths, new_pos, new_latent, new_rope, rate_row,
        positions, jnp.swapaxes(rope_cache, 1, 2), rate_col, in_hbm(latent_cache),
    )

    arrived, keys, cached = lax.optimization_barrier((arrived, keys, cached))
    own = arrived + [blocks[0]]
    other = [hop(v, "core", 1) for v in arrived] + [near]

    B = 1024
    NQ = T * R * HL
    send, keep = pl.pallas_call(
        functools.partial(attend_kernel, (R, J, T, HC, DL, CAP), B),
        out_shape=[
            jax.ShapeDtypeStruct((J, T, R, HC, W), BF),
            jax.ShapeDtypeStruct((J, T, R, HC, W), F32),
        ],
        in_specs=[VMEM] * (2 + 2 * R),
        out_specs=[VMEM, VMEM],
        scratch_shapes=[
            pltpu.VMEM((J, NQ, W), BF),
            pltpu.VMEM((2, NQ, B + LANES), F32),
            pltpu.VMEM((J, NQ, DL), F32),
        ],
        compiler_params=pltpu.CompilerParams(vmem_limit_bytes=16 << 20),
        name="attend",
    )(keys, cached, *own, *other)
    got = hop(send, "core", 1)
    pieces = pl.pallas_call(
        functools.partial(pair_kernel, (R, J, T, HC, HS, CH, DL)),
        out_shape=[jax.ShapeDtypeStruct((R * HB, W), BF if n else F32) for n in range(CH)],
        in_specs=[VMEM, VMEM],
        out_specs=[VMEM] * CH,
        compiler_params=big,
        name="pair",
    )(keep, got)
    shares = hops(pieces, "chip") + [pieces[0]]
    sizes = [HB, HB] + [2 * HB] * (R // 2 - 1)
    latents = pl.pallas_call(
        functools.partial(combine_kernel, (CH, DL)),
        out_shape=[jax.ShapeDtypeStruct((n, DL), BF) for n in sizes],
        in_specs=[VMEM] * CH,
        out_specs=[VMEM] * len(sizes),
        compiler_params=big,
        name="combine",
    )(*shares)
    returned = [
        lax.ppermute(
            latents[1 + i],
            ("req", "core"),
            [(2 * g + c, 2 * (g ^ (2 * i + c)) + c) for g in range(R) for c in range(2)],
        )
        for i in reversed(range(1, R // 2))
    ]
    returned += [hop(latents[1], "req", 1), latents[0]]

    values = pl.pallas_call(
        functools.partial(value_kernel, (R, HC, HS, HB)),
        out_shape=jax.ShapeDtypeStruct((R, HB, DV), BF),
        in_specs=[VMEM] * (1 + len(returned)),
        out_specs=VMEM,
        compiler_params=big,
        name="value",
    )(w_uv, *returned)
    gathered = []
    for n in range(2, CH):
        block = hop(values, "chip", n)
        gathered += [block, hop(block, "core", 1)]
    both = jnp.stack([values, hop(values, "core", 1)])
    gathered += [hop(both, "chip", 1), both]
    return pl.pallas_call(
        functools.partial(place_kernel, (R, J, T, HC, HS, HB, CH)),
        out_shape=jax.ShapeDtypeStruct((T, REQS, HL, DV), BF),
        in_specs=[SMEM] + [VMEM] * len(gathered),
        out_specs=VMEM,
        compiler_params=big,
        name="place",
    )(places, *gathered)


def solution(mesh):
    groups, shards = mesh.shape["req"], mesh.shape["seq"]
    cut = Mesh(mesh.devices.reshape(groups, shards // 2, 2), ("req", "chip", "core"))
    seq = ("chip", "core")
    in_specs = (
        P(None, None, "req", None),
        P(None, None, "req", None),
        P("req", None, None),
        P("req", None, None),
        P("req", seq, None),
        P("req", seq, None),
        P("req", seq),
        P(),
        P(),
        P(),
        P(),
        P(),
    )
    out_specs = P(None, None, "req", None)
    return jax.shard_map(body, mesh=cut, in_specs=in_specs, out_specs=out_specs, check_vma=False)
```
